512 devices in a mesh: blk: 64 (over x, z), grp: 8 (over y, core).
Axes of the slice: x: 4, y: 4, z: 16, core: 2. Of those that a mesh axis runs over, the one named last changes fastest.
Arguments:
- points: bfloat16 [8, 65536, 128], P('grp', 'blk'), may hold values from -4 to 4
- start_panel: bfloat16 [8, 64, 65536], P('grp', None, 'blk'), may hold values from -6 to 6
- seventh: int32 [8, 65536], P('grp', 'blk'), may hold values from 0 to 255, as said below
- neighbours: int32 [8, 256, 16], P('grp'), may hold values from 0 to 255, as said below
- counts: int32 [8, 256], P('grp'), may hold values from 1 to 16, as said below
Outputs:
- ortho_basis: float32 [8, 64, 65536], P('grp', None, 'blk')
- r_factor: float32 [64, 64], replicated
The draws below stay inside these ranges and needn't reach their ends.
Inputs may be any that keep to these rules, and one draw needn't show every extreme that they name: `seventh`: A point's position within its own block, never the point's own position. `neighbours`: block numbers within the group; block B's owner is B // 4. The listed entries of a block are distinct, never the block itself, and each is owned by an owner whose number differs from B's owner by at most 4 modulo 64. The entries after the listed ones are block numbers of the group and are not used. Of the blocks of one owner, at most 2 are listed by the blocks of another owner together, and exactly 2 for some pairs of owners. `counts`: some block of every group lists 16 blocks.
All inputs are finite; a program needn't handle non-finite values.
Results may differ from the reference program's by a relative error of at most 0.0082.
Values may be sent and summed in bfloat16 or wider, within the bound.
A program may use at most 64 MiB of HBM per device.

```python
import math
import jax
import jax.numpy as jnp
from jax import lax

E = 128
K = 64
BS = 256
SLOTS = 16
CAP = 2
REACH = 4
BLK_DEV = 4
GROUPS = 8
OWNERS = 64
GBLOCKS = 256
GROUP_PTS = 65536
POINTS = 524288


def draw_points(key, part):
    key_centre, key_spread, key_column = jax.random.split(key, 3)
    centre = 0.7 * jnp.clip(jax.random.normal(key_centre, (GROUPS, GBLOCKS, 1, E)), -4.0, 4.0)
    spread = 0.3 * jnp.clip(jax.random.normal(key_spread, (GROUPS, GBLOCKS, BS, E)), -4.0, 4.0)
    column_scale = jnp.exp(jax.random.uniform(key_column, (E,), minval=math.log(0.1), maxval=0.0))
    values = (centre + spread) * column_scale
    return values.reshape(GROUPS, GROUP_PTS, E).astype(jnp.bfloat16)


def draw_seventh(key, part):
    step_size = jax.random.randint(key, (GROUPS, GROUP_PTS), 1, BS)
    within = jnp.arange(GROUP_PTS, dtype=jnp.int32) % BS
    return ((within[None, :] + step_size) % BS).astype(jnp.int32)


def draw_neighbours(key, part):
    offsets = jnp.arange(-REACH, REACH + 1, dtype=jnp.int32)
    pool_size = (2 * REACH + 1) * CAP

    def one_group(group_key):
        pool_key, order_key = jax.random.split(group_key)
        pick_keys = jax.random.split(pool_key, OWNERS * (2 * REACH + 1))
        chosen = jax.vmap(lambda each: jax.random.permutation(each, BLK_DEV)[:CAP])(pick_keys)
        chosen = chosen.reshape(OWNERS, 2 * REACH + 1, CAP).astype(jnp.int32)
        targets = (jnp.arange(OWNERS, dtype=jnp.int32)[:, None] + offsets[None, :]) % OWNERS
        pool = (targets[:, :, None] * BLK_DEV + chosen).reshape(OWNERS, pool_size)
        block_pool = jnp.repeat(pool, BLK_DEV, axis=0)
        order_keys = jax.random.split(order_key, GBLOCKS)
        orders = jax.vmap(lambda each: jax.random.permutation(each, pool_size))(order_keys)
        shuffled = jnp.take_along_axis(block_pool, orders.astype(jnp.int32), axis=1)
        selfs = jnp.arange(GBLOCKS, dtype=jnp.int32)
        late = (shuffled == selfs[:, None]).astype(jnp.int32)
        placed = jnp.argsort(late, axis=1, stable=True).astype(jnp.int32)
        return jnp.take_along_axis(shuffled, placed, axis=1)[:, :SLOTS]
    group_keys = jax.random.split(key, GROUPS)
    return jax.vmap(one_group)(group_keys).astype(jnp.int32)


def draw_counts(key, part):
    key_first, key_second, key_full = jax.random.split(key, 3)
    first = jax.random.randint(key_first, (GROUPS, GBLOCKS), 0, SLOTS)
    second = jax.random.randint(key_second, (GROUPS, GBLOCKS), 0, SLOTS)
    lowest = 1 + jnp.minimum(first, second)
    full_at = jax.random.randint(key_full, (GROUPS, 1), 0, GBLOCKS)
    filled = jnp.where(jnp.arange(GBLOCKS, dtype=jnp.int32)[None, :] == full_at, SLOTS, lowest)
    return filled.astype(jnp.int32)


def block_levels(own_key, extent, shards, low, top_value):
    gain = 1.0
    for axis_at, parts in shards:
        draws = jax.random.uniform(jax.random.fold_in(jax.random.fold_in(own_key, 6), axis_at), (parts,), jnp.float32, low / len(shards), top_value / len(shards))
        gain = gain * jnp.repeat(jnp.exp(draws), extent[axis_at] // parts).reshape((-1,) + (1,) * (len(extent) - 1 - axis_at))
    return gain


def gaussian(own_key, shape, scale, reach, shards=(), kind=jnp.bfloat16):
    factor_of = block_levels(own_key, shape, shards, -0.22, 0.18) if shards else 1.0
    array = jax.random.normal(own_key, shape, jnp.float32) * scale * factor_of
    return jnp.minimum(jnp.maximum(array, -reach), reach).astype(kind)


def setup_inputs(seed: int = 0) -> dict:
    key_of = jax.random.split(jax.random.key(seed), 6)
    return {
        "points": draw_points(jax.random.fold_in(key_of[5], 71), 0),
        "start_panel": gaussian(key_of[1], (GROUPS, K, GROUP_PTS), 1.0, 6.0, ((0, 8), (2, 64))),
        "seventh": draw_seventh(jax.random.fold_in(key_of[5], 71), 0),
        "neighbours": draw_neighbours(jax.random.fold_in(key_of[5], 71), 0),
        "counts": draw_counts(jax.random.fold_in(key_of[5], 71), 0),
    }


def group_walk(inputs):
    grp_points, grp_panel, grp_seventh, grp_lists, grp_counts = inputs
    own_points = grp_points.reshape(GBLOCKS, BS, E)
    partner_pos = grp_seventh.reshape(GBLOCKS, BS).astype(jnp.int32)
    partner = jnp.take_along_axis(own_points, partner_pos[:, :, None], axis=1)
    difference = own_points.astype(jnp.float32) - partner.astype(jnp.float32)
    scales = jnp.sqrt(lax.optimization_barrier(jnp.sum(difference * difference, axis=-1)) + 1e-06).astype(jnp.bfloat16)
    as_float = own_points.astype(jnp.float32)
    sq_norm = lax.optimization_barrier(jnp.sum(as_float * as_float, axis=-1))
    panel_grid = grp_panel.reshape(K, GBLOCKS, BS)

    def block_walk(row_blk):
        col_ids = grp_lists[row_blk].astype(jnp.int32)
        live_slots = (jnp.arange(SLOTS) < grp_counts[row_blk]).astype(jnp.float32)
        col_points = own_points[col_ids].astype(jnp.float32)
        col_scales = scales[col_ids].astype(jnp.float32)
        col_norms = sq_norm[col_ids]
        col_panel = panel_grid[:, col_ids].astype(jnp.float32)
        inner_prod = jnp.einsum('pe,sqe->spq', own_points[row_blk].astype(jnp.float32), col_points)
        distance = sq_norm[row_blk][None, :, None] + col_norms[:, None, :] - 2.0 * inner_prod
        denom_scale = scales[row_blk].astype(jnp.float32)[None, :, None] * col_scales[:, None, :]
        affinity = jnp.exp(-distance / denom_scale) * live_slots[:, None, None]
        degree = 1.0 + lax.optimization_barrier(jnp.sum(affinity, axis=(0, 2)))
        weights = affinity.astype(jnp.bfloat16).astype(jnp.float32)
        carried = jnp.einsum('spq,ksq->kp', weights, col_panel)
        return (panel_grid[:, row_blk].astype(jnp.float32) + carried) / degree[None, :]
    walked = lax.map(block_walk, jnp.arange(GBLOCKS))
    return jnp.transpose(walked, (1, 0, 2)).reshape(K, GROUP_PTS)

def reference(points, start_panel, seventh, neighbours, counts):
    walked = lax.map(group_walk, (points, start_panel, seventh, neighbours, counts))
    flat_walk = jnp.transpose(walked, (1, 0, 2)).reshape(K, GROUPS * GROUP_PTS)
    gram_matrix = jnp.dot(flat_walk.astype(jnp.float32), flat_walk.T.astype(jnp.float32), precision=lax.Precision.HIGHEST, preferred_element_type=jnp.float32)
    lower_factor = jnp.linalg.cholesky(gram_matrix)
    solved = lax.linalg.triangular_solve(lower_factor, flat_walk, left_side=True, lower=True)
    root_count = math.sqrt(POINTS)
    ortho_basis = jnp.transpose((solved * root_count).reshape(K, GROUPS, GROUP_PTS), (1, 0, 2))
    r_factor = lower_factor.T / root_count
    return (ortho_basis, r_factor)
```

```python
import functools
import math

import jax
import jax.numpy as jnp
from jax import lax
from jax.experimental import pallas as pl
from jax.experimental.pallas import tpu as pltpu
from jax.sharding import PartitionSpec as P

E = 128
K = 64
BS = 256
SLOTS = 16
REACH = 4
NB = 4
ROWS = BS + 2 * K + 16
KP = K + 16
LOG2E = 1.4426950408889634
MESH = pl.DeviceIdType.MESH
F32 = jnp.float32
BF16 = jnp.bfloat16


def nt_dot(a, b, precision=None):
    return lax.dot_general(
        a, b, (((1,), (1,)), ((), ())), precision=precision, preferred_element_type=F32
    )


def split3(value):
    hi = value.astype(BF16).astype(F32)
    mid = (value - hi).astype(BF16).astype(F32)
    return hi, mid, value - hi - mid


def walk_kernel(
    sizes, pts, pan, sev, lists, counts, walked, gram_out,
    own, recv, xaug, apcol, acc, mask, gram, part, stage_a, stage_b, stage_c, full,
    ssem, rsem, asend, arecv,
):
    nb, ng, fb, hops = sizes
    fc = nb // fb
    steps = NB * hops
    me = lax.axis_index("blk")
    mg = lax.axis_index("grp")
    right = lax.rem(me + 1, nb)
    left = lax.rem(me + nb - 1, nb)
    lo = lax.rem(me, fb)
    high = me // fb

    def grp_peer(o):
        return lax.rem(mg + o, ng)

    def b_peer(o):
        return high * fb + lax.rem(lo + o, fb)

    def c_peer(o):
        return lax.rem(high + o, fc) * fb + lo

    partners = [(right, mg), (left, mg)]
    partners += [(me, grp_peer(o)) for o in range(1, ng)]
    partners += [(b_peer(o), mg) for o in range(1, fb)]
    partners += [(c_peer(o), mg) for o in range(1, fc)]
    barrier = pltpu.get_barrier_semaphore()
    for partner in partners:
        pl.semaphore_signal(barrier, inc=1, device_id=partner, device_id_type=MESH)

    lane = lax.broadcasted_iota(jnp.int32, (BS, E), 1)

    def prepare(b):
        cols = slice(b * BS, (b + 1) * BS)
        x = pts[0, cols, :]
        xf = x.astype(F32)
        place = jnp.broadcast_to(sev[0:1, cols].astype(F32), (E, BS)).T
        place = jnp.concatenate([place, place], axis=1).astype(jnp.int32)
        picked = (place == lax.broadcasted_iota(jnp.int32, (BS, BS), 1)).astype(F32).astype(BF16)
        partner = jnp.dot(picked, x, preferred_element_type=F32)
        diff = xf - partner
        scale = jnp.sqrt(jnp.sum(diff * diff, axis=1, keepdims=True) + 1e-06)
        scale = jnp.broadcast_to(scale, (BS, E)).astype(BF16).astype(F32)
        norm = jnp.broadcast_to(jnp.sum(xf * xf, axis=1, keepdims=True), (BS, E))
        hi, mid, low = split3(norm)
        zero = jnp.zeros_like(norm)
        stats = jnp.where(
            lane == 0, scale, jnp.where(lane == 1, hi, jnp.where(lane == 2, mid, jnp.where(lane == 3, low, zero)))
        ).T[0:8, :]
        own[b, 0:BS, :] = x
        own[b, BS : BS + K, :] = pan[0, :, b * BS : b * BS + E]
        own[b, BS + K : BS + 2 * K, :] = pan[0, :, b * BS + E : (b + 1) * BS]
        own[b, BS + 2 * K : ROWS, :] = jnp.concatenate([stats[:, :E], stats[:, E:]], axis=0).astype(BF16)
        extra = jnp.where(lane == 0, -hi, jnp.where(lane == 1, -mid, jnp.where(lane == 2, -low, zero)))
        xaug[b, :, 0:E] = (2.0 * xf).astype(BF16)
        xaug[b, :, E : 2 * E] = extra.astype(BF16)
        apcol[b, :, :] = LOG2E / scale

    def hop(d, slot, source):
        return pltpu.make_async_remote_copy(
            src_ref=source,
            dst_ref=recv.at[d, slot],
            send_sem=ssem.at[d, slot],
            recv_sem=rsem.at[d, slot],
            device_id=((right, left)[d], mg),
            device_id_type=MESH,
        )

    prepare(0)
    pl.semaphore_wait(barrier, len(partners))
    for b in range(NB):
        if b:
            prepare(b)
        for d in range(2):
            hop(d, b, own.at[b]).start()

    spot = lax.broadcasted_iota(jnp.int32, mask.shape[1:], 0)
    away = spot - NB
    second = away >= steps
    away = jnp.where(second, away - steps, away)
    dist = lax.shift_right_arithmetic(away, 2) + 1
    owner = me + jnp.where(second, dist, -dist)
    owner = jnp.where(owner < 0, owner + nb, jnp.where(owner >= nb, owner - nb, owner))
    ids = jnp.where(spot < NB, me, owner) * NB + (away & (NB - 1))
    for r in range(NB):
        row = me * NB + r
        found = jnp.zeros(ids.shape, jnp.int32)
        for s in range(SLOTS):
            entry = jnp.where(s < counts[0, row], lists[0, row, s], -1)
            found = jnp.where(ids == entry, 1, found)
        mask[r, :, :] = found

    acc[...] = jnp.zeros_like(acc)
    tail = (lane < 3).astype(F32).astype(BF16)
    ones = jnp.ones((KP - K, BS), BF16)

    def block(slab, spot_index):
        keys = jnp.concatenate([slab[0:BS, :], tail], axis=1)
        panel = jnp.concatenate([slab[BS : BS + K, :], slab[BS + K : BS + 2 * K, :]], axis=1)
        panel = jnp.concatenate([panel, ones], axis=0)
        stats = slab[BS + 2 * K : ROWS, :].astype(F32)
        stats = jnp.concatenate([stats[0:8, :], stats[8:16, :]], axis=1)
        aq = 1.0 / stats[0:1, :]
        nq = stats[1:2, :] + stats[2:3, :] + stats[3:4, :]
        for r in range(NB):
            cross = nt_dot(xaug[r], keys)
            ap = apcol[r]
            power = ((cross - nq) * aq) * jnp.concatenate([ap, ap], axis=1)
            weights = jnp.exp2(power).astype(BF16)
            carried = nt_dot(panel, weights)
            live = mask[r, pl.ds(spot_index, 1), :]
            live = jnp.concatenate([live, live], axis=1)
            acc[r, :, :] += jnp.where(live > 0, carried, 0.0)

    for b in range(NB):
        block(own.at[b], b)

    def arrive(t, carry):
        for d in range(2):
            hop(d, t, recv.at[d, t]).wait_recv()

            @pl.when(t < steps - NB)
            def _():
                hop(d, t + NB, recv.at[d, t]).start()

        for d in range(2):
            block(recv.at[d, t], NB + d * steps + t)
        return carry

    lax.fori_loop(0, steps, arrive, 0)

    for r in range(NB):
        cols = slice(r * BS, (r + 1) * BS)
        total = acc[r, :, :]
        walked[:, cols] = (pan[0, :, cols].astype(F32) + total[0:K, :]) / (1.0 + total[K : K + 1, :])
    flat = walked[...]
    gram[...] = jnp.concatenate(
        [nt_dot(flat, flat, lax.Precision.HIGHEST), jnp.zeros((K, E - K), F32)], axis=1
    )

    def sent(t, carry):
        for d in range(2):
            hop(d, t, recv.at[d, t]).wait_send()
        return carry

    share = K // ng

    def exchange(stage, size, source, target, peer):
        copies = []
        for o in range(1, size):
            copy = pltpu.make_async_remote_copy(
                src_ref=source(o),
                dst_ref=target,
                send_sem=asend.at[stage, o - 1],
                recv_sem=arecv.at[stage, o - 1],
                device_id=peer(o),
                device_id_type=MESH,
            )
            copy.start()
            copies.append(copy)
        return copies

    def summed(slots, size):
        total = slots[0]
        for i in range(1, size):
            total = total + slots[i]
        return total

    def mine(o):
        start = pl.multiple_of(grp_peer(o) * share, share)
        return gram.at[pl.ds(start, share), :]

    copies = exchange(0, ng, mine, stage_a.at[mg], lambda o: (me, grp_peer(o)))
    own_rows = pl.ds(pl.multiple_of(mg * share, share), share)
    stage_a[mg] = gram[own_rows, :]
    lax.fori_loop(0, steps, sent, 0)
    for copy in copies:
        copy.wait()
    part[0] = summed(stage_a, ng)
    copies = exchange(1, fb, lambda o: part.at[0], stage_b.at[lo], lambda o: (b_peer(o), mg))
    stage_b[lo] = part[0]
    for copy in copies:
        copy.wait()
    part[1] = summed(stage_b, fb)
    copies = exchange(2, fc, lambda o: part.at[1], stage_c.at[high], lambda o: (c_peer(o), mg))
    stage_c[high] = part[1]
    for copy in copies:
        copy.wait()
    part[2] = summed(stage_c, fc)
    copies = exchange(3, ng, lambda o: part.at[2], full.at[mg], lambda o: (me, grp_peer(o)))
    full[mg] = part[2]
    for copy in copies:
        copy.wait()
    for i in range(ng):
        gram_out[i * share : (i + 1) * share, :] = full[i]


def solve_kernel(root, gram, walked, ortho, r_factor):
    group = 8
    sub = lax.broadcasted_iota(jnp.int32, (group, E), 0)
    col = lax.broadcasted_iota(jnp.int32, (group, E), 1)
    tiles = []
    for i in range(K // group):
        unit = (col == sub + (K + i * group)).astype(F32)
        tiles.append(gram[i * group : (i + 1) * group, :] + unit)
    for j in range(K):
        at, inner = divmod(j, group)
        row = tiles[at][inner : inner + 1, :]
        row = row * (1.0 / row[:, j : j + 1])
        for i in range(at, K // group):
            factor = tiles[i][:, j : j + 1]
            if i == at:
                factor = jnp.where(sub[:, 0:1] > inner, factor, 0.0)
            tiles[i] = tiles[i] - factor * row
    inverse = []
    for i in range(K // group):
        diagonal = jnp.sum(jnp.where(col == sub + i * group, tiles[i], 0.0), axis=1, keepdims=True)
        scaled = tiles[i] * (1.0 / jnp.sqrt(diagonal))
        upper = jnp.where(col >= sub + i * group, scaled, 0.0)
        r_factor[i * group : (i + 1) * group, :] = upper[:, 0:K] * (1.0 / root)
        inverse.append(scaled[:, K : 2 * K] * root)
    inverse = jnp.concatenate(inverse, axis=0)
    ortho[0, :, :] = jnp.dot(
        inverse, walked[...], precision=lax.Precision.HIGHEST, preferred_element_type=F32
    )


def local(points, start_panel, seventh, neighbours, counts):
    nb = lax.axis_size("blk")
    ng = lax.axis_size("grp")
    fb = 2 ** ((nb.bit_length() - 1) // 2)
    hops = min(REACH, (nb - 1) // 2)
    pts = points.shape[1]
    share = K // ng
    steps = NB * hops
    vmem = pl.BlockSpec(memory_space=pltpu.VMEM)
    smem = pl.BlockSpec(memory_space=pltpu.SMEM)
    widest = max(ng, fb, nb // fb)
    walked, gram = pl.pallas_call(
        functools.partial(walk_kernel, (nb, ng, fb, hops)),
        out_shape=(
            jax.ShapeDtypeStruct((K, pts), F32),
            jax.ShapeDtypeStruct((K, E), F32),
        ),
        in_specs=[vmem, vmem, vmem, smem, smem],
        out_specs=(vmem, vmem),
        scratch_shapes=[
            pltpu.VMEM((NB, ROWS, E), BF16),
            pltpu.VMEM((2, steps, ROWS, E), BF16),
            pltpu.VMEM((NB, BS, 2 * E), BF16),
            pltpu.VMEM((NB, BS, E), F32),
            pltpu.VMEM((NB, KP, BS), F32),
            pltpu.VMEM((NB, 40, E), jnp.int32),
            pltpu.VMEM((K, E), F32),
            pltpu.VMEM((3, share, E), F32),
            pltpu.VMEM((ng, share, E), F32),
            pltpu.VMEM((fb, share, E), F32),
            pltpu.VMEM((nb // fb, share, E), F32),
            pltpu.VMEM((ng, share, E), F32),
            pltpu.SemaphoreType.DMA((2, steps)),
            pltpu.SemaphoreType.DMA((2, steps)),
            pltpu.SemaphoreType.DMA((4, widest)),
            pltpu.SemaphoreType.DMA((4, widest)),
        ],
        compiler_params=pltpu.CompilerParams(
            collective_id=0, has_side_effects=True, vmem_limit_bytes=32 * 1024 * 1024
        ),
        name="walk",
    )(points, start_panel, seventh, neighbours, counts)
    root = math.sqrt(pts * nb * ng)
    return pl.pallas_call(
        functools.partial(solve_kernel, root),
        out_shape=(
            jax.ShapeDtypeStruct((1, K, pts), F32),
            jax.ShapeDtypeStruct((K, K), F32),
        ),
        in_specs=[vmem, vmem],
        out_specs=(vmem, vmem),
        name="solve",
    )(gram, walked)


def solution(mesh):
    in_specs = (
        P("grp", "blk", None),
        P("grp", None, "blk"),
        P("grp", "blk"),
        P("grp", None, None),
        P("grp", None),
    )
    out_specs = (P("grp", None, "blk"), P())
    return jax.shard_map(local, mesh=mesh, in_specs=in_specs, out_specs=out_specs, check_vma=False)
```

```python
import functools
import math

import jax
import jax.numpy as jnp
from jax import lax
from jax.experimental import pallas as pl
from jax.experimental.pallas import tpu as pltpu
from jax.sharding import PartitionSpec as P

E = 128
K = 64
BS = 256
SLOTS = 16
REACH = 4
NB = 4
ROWS = BS + 2 * K + 16
KP = K + 16
LOG2E = 1.4426950408889634
MESH = pl.DeviceIdType.MESH
F32 = jnp.float32
BF16 = jnp.bfloat16


def nt_dot(a, b, precision=None):
    return lax.dot_general(
        a, b, (((1,), (1,)), ((), ())), precision=precision, preferred_element_type=F32
    )


def split3(value):
    hi = value.astype(BF16).astype(F32)
    mid = (value - hi).astype(BF16).astype(F32)
    return hi, mid, value - hi - mid


def far_slots(listed):
    f0, f1, f2, f3 = listed
    n0, n1, n2, n3 = 1 - f0, 1 - f1, 1 - f2, 1 - f3
    first = (f0, n0 * f1, n0 * n1 * f2 * f3, jnp.zeros_like(f0))
    second = (jnp.zeros_like(f0), n3 * n2 * f1 * f0, n3 * f2, f3)
    return first, second


def walk_kernel(
    sizes, pts, pan, sev, lists, counts, walked, gram_out,
    own, recv, stage, xaug, apcol, acc, mask, pick, g3, s0, s1, s2, p3,
    isem, ssem, rsem, asend, arecv,
):
    nb, ng, nz, hops = sizes
    nx = nb // nz
    near = NB * (hops - 1)
    steps = near + 2
    me = lax.axis_index("blk")
    mg = lax.axis_index("grp")
    right = lax.rem(me + 1, nb)
    left = lax.rem(me + nb - 1, nb)
    zz = lax.rem(me, nz)
    xx = me // nz
    team = nx * ng
    rank = xx * ng + mg

    def team_peer(o):
        at = lax.rem(rank + o, team)
        return ((at // ng) * nz + zz, lax.rem(at, ng)), at

    def line_peer(o):
        return (xx * nz + lax.rem(zz + o, nz), mg)

    loads = []
    for b in range(NB):
        low = b * BS
        loads.append(
            [
                pltpu.make_async_copy(pts.at[0, low : low + BS, :], own.at[b, 0:BS, :], isem.at[b, 0]),
                pltpu.make_async_copy(
                    pan.at[0, :, low : low + E], own.at[b, BS : BS + K, :], isem.at[b, 1]
                ),
                pltpu.make_async_copy(
                    pan.at[0, :, low + E : low + BS], own.at[b, BS + K : BS + 2 * K, :], isem.at[b, 2]
                ),
            ]
        )
        for load in loads[b]:
            load.start()

    partners = [(right, mg), (left, mg)]
    partners += [team_peer(o)[0] for o in range(1, team)]
    partners += [line_peer(o) for o in range(1, nz)]
    barrier = pltpu.get_barrier_semaphore()
    for partner in partners:
        pl.semaphore_signal(barrier, inc=1, device_id=partner, device_id_type=MESH)

    lane = lax.broadcasted_iota(jnp.int32, (BS, E), 1)

    def prepare(b):
        for load in loads[b]:
            load.wait()
        x = own[b, 0:BS, :]
        xf = x.astype(F32)
        place = jnp.broadcast_to(sev[0:1, b * BS : (b + 1) * BS].astype(F32), (E, BS)).T
        place = jnp.concatenate([place, place], axis=1).astype(jnp.int32)
        picked = (place == lax.broadcasted_iota(jnp.int32, (BS, BS), 1)).astype(F32).astype(BF16)
        partner = jnp.dot(picked, x, preferred_element_type=F32)
        diff = xf - partner
        scale = jnp.sqrt(jnp.sum(diff * diff, axis=1, keepdims=True) + 1e-06)
        scale = jnp.broadcast_to(scale, (BS, E)).astype(BF16).astype(F32)
        norm = jnp.broadcast_to(jnp.sum(xf * xf, axis=1, keepdims=True), (BS, E))
        hi, mid, low = split3(norm)
        zero = jnp.zeros_like(norm)
        stats = jnp.where(
            lane == 0, scale, jnp.where(lane == 1, hi, jnp.where(lane == 2, mid, jnp.where(lane == 3, low, zero)))
        ).T[0:8, :]
        own[b, BS + 2 * K : ROWS, :] = jnp.concatenate([stats[:, :E], stats[:, E:]], axis=0).astype(BF16)
        extra = jnp.where(lane == 0, -hi, jnp.where(lane == 1, -mid, jnp.where(lane == 2, -low, zero)))
        xaug[b, :, 0:E] = (2.0 * xf).astype(BF16)
        xaug[b, :, E : 2 * E] = extra.astype(BF16)
        apcol[b, :, :] = LOG2E / scale

    def hop(d, slot, source):
        return pltpu.make_async_remote_copy(
            src_ref=source,
            dst_ref=recv.at[d, slot],
            send_sem=ssem.at[d, slot],
            recv_sem=rsem.at[d, slot],
            device_id=((right, left)[d], mg),
            device_id_type=MESH,
        )

    prepare(0)
    pl.semaphore_wait(barrier, len(partners))
    for b in range(NB):
        if b:
            prepare(b)
        for d in range(2):
            hop(d, b, own.at[b]).start()

    def wrapped(owner):
        return jnp.where(owner < 0, owner + nb, jnp.where(owner >= nb, owner - nb, owner))

    def found_in(ids, row, found):
        for s in range(SLOTS):
            entry = jnp.where(s < counts[0, row], lists[0, s, row], -1)
            found = jnp.where(ids == entry, 1, found)
        return found

    far = NB + 2 * near
    spot = lax.broadcasted_iota(jnp.int32, (mask.shape[1], E), 0)
    away = spot - NB
    second_half = away >= near
    dist = lax.shift_right_arithmetic(jnp.where(second_half, away - near, away), 2) + 1
    shift = jnp.where(second_half, dist, -dist)
    shift = jnp.where(spot >= far, jnp.where(spot >= far + NB, hops, -hops), shift)
    shift = jnp.where(spot < NB, 0, shift)
    ids = wrapped(me + shift) * NB + (spot & (NB - 1))
    founds = []
    for r in range(NB):
        found = found_in(ids, me * NB + r, jnp.zeros(ids.shape, jnp.int32))
        founds.append(found)
        mask[r, :, :] = found
    for d in range(2):
        rows = [[f[far + NB * d + c : far + NB * d + c + 1, :] for c in range(NB)] for f in founds]
        listed = [functools.reduce(jnp.maximum, [row[c] for row in rows]) for c in range(NB)]
        for at, chosen in enumerate(far_slots(listed)):
            for r in range(NB):
                live = sum(chosen[c] * rows[r][c] for c in range(NB))
                mask[r, far + 2 * d + at : far + 2 * d + at + 1, :] = live
    sub = lax.broadcasted_iota(jnp.int32, (8, E), 0)
    for d in range(2):
        toward = (right, left)[d]
        source = wrapped(me + (1 - hops, hops - 1)[d])
        blocks = source * NB + sub
        found = jnp.zeros((8, E), jnp.int32)
        for r in range(NB):
            found = found_in(blocks, toward * NB + r, found)
        for at, chosen in enumerate(far_slots([found[c : c + 1, :] for c in range(NB)])):
            for c in range(NB):
                pick[d, at, c, :, :] = chosen[c]

    acc[...] = jnp.zeros_like(acc)
    stage[...] = jnp.zeros_like(stage)
    tail = (lane < 3).astype(F32).astype(BF16)
    ones = jnp.ones((KP - K, BS), BF16)

    def block(slab, spot_index):
        keys = jnp.concatenate([slab[0:BS, :], tail], axis=1)
        panel = jnp.concatenate([slab[BS : BS + K, :], slab[BS + K : BS + 2 * K, :]], axis=1)
        panel = jnp.concatenate([panel, ones], axis=0)
        stats = slab[BS + 2 * K : ROWS, :].astype(F32)
        stats = jnp.concatenate([stats[0:8, :], stats[8:16, :]], axis=1)
        aq = 1.0 / stats[0:1, :]
        nq = stats[1:2, :] + stats[2:3, :] + stats[3:4, :]
        for r in range(NB):
            cross = nt_dot(xaug[r], keys)
            ap = apcol[r]
            power = ((cross - nq) * aq) * jnp.concatenate([ap, ap], axis=1)
            weights = jnp.exp2(power).astype(BF16)
            carried = nt_dot(panel, weights)
            live = mask[r, pl.ds(spot_index, 1), :]
            live = jnp.concatenate([live, live], axis=1)
            acc[r, :, :] += jnp.where(live > 0, carried, 0.0)

    def inside(b, carry):
        block(own.at[b], b)
        return carry

    lax.fori_loop(0, NB, inside, 0)

    def arrive(t, carry):
        last = t - (near - NB)
        for d in range(2):
            hop(d, t, recv.at[d, t]).wait_recv()

            @pl.when(t < near - NB)
            def _():
                hop(d, t + NB, recv.at[d, t]).start()

            for at, (low, high) in enumerate(((0, 2), (1, 3))):

                @pl.when(jnp.logical_and(last >= low, last <= high))
                def _():
                    wanted = pick[d, at, last]
                    kept = stage[d, at].astype(F32)
                    taken = jnp.where(wanted > 0, recv[d, t].astype(F32), kept)
                    stage[d, at] = taken.astype(BF16)

                @pl.when(last == high)
                def _():
                    hop(d, near + at, stage.at[d, at]).start()

        for d in range(2):
            block(recv.at[d, t], NB + d * near + t)
        return carry

    lax.fori_loop(0, near, arrive, 0)

    def arrive_far(t, carry):
        for d in range(2):
            hop(d, near + t, recv.at[d, near + t]).wait_recv()
        for d in range(2):
            block(recv.at[d, near + t], far + 2 * d + t)
        return carry

    lax.fori_loop(0, 2, arrive_far, 0)

    for r in range(NB):
        cols = slice(r * BS, (r + 1) * BS)
        total = acc[r, :, :]
        panel = jnp.concatenate([own[r, BS : BS + K, :], own[r, BS + K : BS + 2 * K, :]], axis=1)
        walked[:, cols] = (panel.astype(F32) + total[0:K, :]) / (1.0 + total[K : K + 1, :])
    flat = walked[...]
    gram = jnp.concatenate(
        [nt_dot(flat, flat, lax.Precision.HIGHEST), jnp.zeros((K, E - K), F32)], axis=1
    )

    def sent(t, carry):
        for d in range(2):
            hop(d, t, recv.at[d, t]).wait_send()
        return carry

    share = K // team

    def exchange(at, size, source, target, slot, peer):
        for o in range(1, size):
            pltpu.make_async_remote_copy(
                src_ref=source(o),
                dst_ref=target.at[slot],
                send_sem=asend.at[at],
                recv_sem=arecv.at[at],
                device_id=peer(o),
                device_id_type=MESH,
            ).start()

    def arrived(at, size, target):
        whole = target.at[pl.ds(0, size - 1)]
        return pltpu.make_async_remote_copy(
            src_ref=whole,
            dst_ref=whole,
            send_sem=asend.at[at],
            recv_sem=arecv.at[at],
            device_id=line_peer(1),
            device_id_type=MESH,
        )

    for i in range(team):
        g3[i] = gram[i * share : (i + 1) * share, :]
    exchange(0, team, lambda o: g3.at[team_peer(o)[1]], s0, rank, lambda o: team_peer(o)[0])
    s0[rank] = g3[rank]
    lax.fori_loop(0, steps, sent, 0)
    arrived(0, team, s0).wait_recv()
    p3[0] = jnp.sum(s0[...], axis=0)
    exchange(1, nz, lambda o: p3.at[0], s1, zz, line_peer)
    s1[zz] = p3[0]
    arrived(1, nz, s1).wait_recv()
    p3[1] = jnp.sum(s1[...], axis=0)
    exchange(2, team, lambda o: p3.at[1], s2, rank, lambda o: team_peer(o)[0])
    s2[rank] = p3[1]
    arrived(2, team, s2).wait_recv()
    for i in range(team):
        gram_out[i * share : (i + 1) * share, :] = s2[i]
    arrived(0, team, s0).wait_send()
    arrived(1, nz, s1).wait_send()
    arrived(2, team, s2).wait_send()


def solve_kernel(root, gram, walked, ortho, r_factor):
    group = 8
    count = K // group
    sub = lax.broadcasted_iota(jnp.int32, (group, E), 0)
    col = lax.broadcasted_iota(jnp.int32, (group, E), 1)
    tiles = []
    for i in range(count):
        unit = (col == sub + (K + i * group)).astype(F32)
        tiles.append(gram[i * group : (i + 1) * group, :] + unit)
    for at in range(count):
        base = at * group
        wide = {
            i: [jnp.broadcast_to(tiles[i][:, base + k : base + k + 1], (group, E)) for k in range(group)]
            for i in range(at, count)
        }
        for k in range(group):
            inverse = 1.0 / wide[at][k][k : k + 1, :]
            row = tiles[at][k : k + 1, :] * inverse
            later = {m: wide[at][m][k : k + 1, :] * inverse for m in range(k + 1, group)}
            for i in range(at, count):
                factor = wide[i][k]
                if i == at:
                    factor = jnp.where(sub > k, factor, 0.0)
                tiles[i] = tiles[i] - factor * row
                for m, value in later.items():
                    wide[i][m] = wide[i][m] - factor * value
    rows = []
    for i in range(count):
        diagonal = jnp.sum(jnp.where(col == sub + i * group, tiles[i], 0.0), axis=1, keepdims=True)
        scaled = tiles[i] * (1.0 / jnp.sqrt(diagonal))
        upper = jnp.where(col >= sub + i * group, scaled, 0.0)
        r_factor[i * group : (i + 1) * group, :] = upper[:, 0:K] * (1.0 / root)
        rows.append(scaled[:, K : 2 * K] * root)
    ortho[0, :, :] = jnp.dot(
        jnp.concatenate(rows, axis=0),
        walked[...],
        precision=lax.Precision.HIGHEST,
        preferred_element_type=F32,
    )


def local(points, start_panel, seventh, neighbours, counts):
    nb = lax.axis_size("blk")
    ng = lax.axis_size("grp")
    nz = max(nb // 4, 1)
    hops = min(REACH, (nb - 1) // 2)
    pts = points.shape[1]
    team = (nb // nz) * ng
    share = K // team
    steps = NB * (hops - 1) + 2
    vmem = pl.BlockSpec(memory_space=pltpu.VMEM)
    smem = pl.BlockSpec(memory_space=pltpu.SMEM)
    hbm = pl.BlockSpec(memory_space=pltpu.HBM)
    walked, gram = pl.pallas_call(
        functools.partial(walk_kernel, (nb, ng, nz, hops)),
        out_shape=(
            jax.ShapeDtypeStruct((K, pts), F32),
            jax.ShapeDtypeStruct((K, E), F32),
        ),
        in_specs=[hbm, hbm, vmem, smem, smem],
        out_specs=(vmem, vmem),
        scratch_shapes=[
            pltpu.VMEM((NB, ROWS, E), BF16),
            pltpu.VMEM((2, steps, ROWS, E), BF16),
            pltpu.VMEM((2, 2, ROWS, E), BF16),
            pltpu.VMEM((NB, BS, 2 * E), BF16),
            pltpu.VMEM((NB, BS, E), F32),
            pltpu.VMEM((NB, KP, BS), F32),
            pltpu.VMEM((NB, 40, E), jnp.int32),
            pltpu.VMEM((2, 2, NB, 1, E), jnp.int32),
            pltpu.VMEM((team, share, E), F32),
            pltpu.VMEM((team, share, E), F32),
            pltpu.VMEM((nz, share, E), F32),
            pltpu.VMEM((team, share, E), F32),
            pltpu.VMEM((2, share, E), F32),
            pltpu.SemaphoreType.DMA((NB, 3)),
            pltpu.SemaphoreType.DMA((2, steps)),
            pltpu.SemaphoreType.DMA((2, steps)),
            pltpu.SemaphoreType.DMA((3,)),
            pltpu.SemaphoreType.DMA((3,)),
        ],
        compiler_params=pltpu.CompilerParams(
            collective_id=0, has_side_effects=True, vmem_limit_bytes=32 * 1024 * 1024
        ),
        name="walk",
    )(
        pltpu.with_memory_space_constraint(points, pltpu.HBM),
        pltpu.with_memory_space_constraint(start_panel, pltpu.HBM),
        seventh,
        jnp.swapaxes(neighbours, 1, 2),
        counts,
    )
    root = math.sqrt(pts * nb * ng)
    return pl.pallas_call(
        functools.partial(solve_kernel, root),
        out_shape=(
            jax.ShapeDtypeStruct((1, K, pts), F32),
            jax.ShapeDtypeStruct((K, K), F32),
        ),
        in_specs=[vmem, vmem],
        out_specs=(vmem, vmem),
        compiler_params=pltpu.CompilerParams(vmem_limit_bytes=16 * 1024 * 1024),
        name="solve",
    )(gram, walked)


def solution(mesh):
    in_specs = (
        P("grp", "blk", None),
        P("grp", None, "blk"),
        P("grp", "blk"),
        P("grp", None, None),
        P("grp", None),
    )
    out_specs = (P("grp", None, "blk"), P())
    return jax.shard_map(local, mesh=mesh, in_specs=in_specs, out_specs=out_specs, check_vma=False)
```

```python
import functools
import math

import jax
import jax.numpy as jnp
from jax import lax
from jax.experimental import pallas as pl
from jax.experimental.pallas import tpu as pltpu
from jax.sharding import PartitionSpec as P

E = 128
K = 64
BS = 256
SLOTS = 16
REACH = 4
NB = 4
ROWS = BS + 2 * K + 16
KP = K + 16
LOG2E = 1.4426950408889634
MESH = pl.DeviceIdType.MESH
F32 = jnp.float32
BF16 = jnp.bfloat16


def nt_dot(a, b, precision=None):
    return lax.dot_general(
        a, b, (((1,), (1,)), ((), ())), precision=precision, preferred_element_type=F32
    )


def split3(value):
    hi = value.astype(BF16).astype(F32)
    mid = (value - hi).astype(BF16).astype(F32)
    return hi, mid, value - hi - mid


def far_slots(listed):
    f0, f1, f2, f3 = listed
    n0, n1, n2, n3 = 1 - f0, 1 - f1, 1 - f2, 1 - f3
    first = (f0, n0 * f1, n0 * n1 * f2 * f3, jnp.zeros_like(f0))
    second = (jnp.zeros_like(f0), n3 * n2 * f1 * f0, n3 * f2, f3)
    return first, second


def walk_kernel(
    sizes, pts, pan, sev_in, lists_in, counts_in, walked, gram_out,
    sev, lists, counts, own, recv, stage, xaug, apcol, acc, mask, pick, g3, s0, s1, s2, p3,
    isem, ssem, rsem, asend, arecv, heard,
):
    nb, ng, nz, hops = sizes
    nx = nb // nz
    near = NB * (hops - 1)
    steps = near + 2
    me = lax.axis_index("blk")
    mg = lax.axis_index("grp")
    right = lax.rem(me + 1, nb)
    left = lax.rem(me + nb - 1, nb)
    zz = lax.rem(me, nz)
    xx = me // nz
    team = nx * ng
    rank = xx * ng + mg

    yy = mg // 2
    core = lax.rem(mg, 2)
    ny = ng // 2

    def team_peer(o):
        gx = lax.rem(xx + o[0], nx)
        gg = lax.rem(yy + o[1], ny) * 2 + lax.rem(core + o[2], 2)
        return (gx * nz + zz, gg), gx * ng + gg

    def line_peer(o):
        return (xx * nz + lax.rem(zz + o, nz), mg)

    def away_by(o, size):
        return min(o, size - o)

    team_offsets = [(a, b, c) for a in range(nx) for b in range(ny) for c in range(2)][1:]
    team_offsets.sort(key=lambda o: (-away_by(o[0], nx) - away_by(o[1], ny), o))
    line_offsets = sorted(range(1, nz), key=lambda o: (-away_by(o, nz), o))

    small = [
        pltpu.make_async_copy(sev_in, sev, isem.at[0, 3]),
        pltpu.make_async_copy(lists_in.at[0], lists, isem.at[1, 3]),
        pltpu.make_async_copy(counts_in, counts, isem.at[2, 3]),
    ]
    small[0].start()
    loads = []
    for b in range(NB):
        low = b * BS
        loads.append(
            [
                pltpu.make_async_copy(pts.at[0, low : low + BS, :], own.at[b, 0:BS, :], isem.at[b, 0]),
                pltpu.make_async_copy(
                    pan.at[0, :, low : low + E], own.at[b, BS : BS + K, :], isem.at[b, 1]
                ),
                pltpu.make_async_copy(
                    pan.at[0, :, low + E : low + BS], own.at[b, BS + K : BS + 2 * K, :], isem.at[b, 2]
                ),
            ]
        )
        for load in loads[b]:
            load.start()

    small[1].start()
    small[2].start()

    next_to = [line_peer(1), line_peer(nz - 1)]
    next_to += [team_peer(o)[0] for o in ((1, 0, 0), (nx - 1, 0, 0), (0, 1, 0), (0, ny - 1, 0), (0, 0, 1))]
    partners = [(right, mg), (left, mg)] + next_to
    rounds = [
        next_to,
        [line_peer(2), line_peer(nz - 2)]
        + [team_peer(o)[0] for o in ((2, 0, 0), (0, 2, 0), (1, 0, 0), (nx - 1, 0, 0))],
        [line_peer(4), line_peer(nz - 4), team_peer((0, 0, 1))[0]],
    ]

    def vouch(at):
        for partner in rounds[at]:
            pl.semaphore_signal(heard.at[at], inc=1, device_id=partner, device_id_type=MESH)

    def hear(at):
        pl.semaphore_wait(heard.at[at], len(rounds[at]))

    barrier = pltpu.get_barrier_semaphore()
    for partner in partners:
        pl.semaphore_signal(barrier, inc=1, device_id=partner, device_id_type=MESH)

    lane = lax.broadcasted_iota(jnp.int32, (BS, E), 1)

    def prepare(b):
        for load in loads[b]:
            load.wait()
        x = own[b, 0:BS, :]
        xf = x.astype(F32)
        place = jnp.broadcast_to(sev[0:1, b * BS : (b + 1) * BS].astype(F32), (E, BS)).T
        place = jnp.concatenate([place, place], axis=1).astype(jnp.int32)
        picked = (place == lax.broadcasted_iota(jnp.int32, (BS, BS), 1)).astype(F32).astype(BF16)
        partner = jnp.dot(picked, x, preferred_element_type=F32)
        diff = xf - partner
        scale = jnp.sqrt(jnp.sum(diff * diff, axis=1, keepdims=True) + 1e-06)
        scale = jnp.broadcast_to(scale, (BS, E)).astype(BF16).astype(F32)
        norm = jnp.broadcast_to(jnp.sum(xf * xf, axis=1, keepdims=True), (BS, E))
        hi, mid, low = split3(norm)
        zero = jnp.zeros_like(norm)
        stats = jnp.where(
            lane == 0, scale, jnp.where(lane == 1, hi, jnp.where(lane == 2, mid, jnp.where(lane == 3, low, zero)))
        ).T[0:8, :]
        own[b, BS + 2 * K : ROWS, :] = jnp.concatenate([stats[:, :E], stats[:, E:]], axis=0).astype(BF16)
        extra = jnp.where(lane == 0, -hi, jnp.where(lane == 1, -mid, jnp.where(lane == 2, -low, zero)))
        xaug[b, :, 0:E] = (2.0 * xf).astype(BF16)
        xaug[b, :, E : 2 * E] = extra.astype(BF16)
        apcol[b, :, :] = LOG2E / scale

    def hop(d, slot, source):
        return pltpu.make_async_remote_copy(
            src_ref=source,
            dst_ref=recv.at[d, slot],
            send_sem=ssem.at[d, slot],
            recv_sem=rsem.at[d, slot],
            device_id=((right, left)[d], mg),
            device_id_type=MESH,
        )

    small[0].wait()
    prepare(0)
    pl.semaphore_wait(barrier, len(partners))
    for b in range(NB):
        if b:
            prepare(b)
        for d in range(2):
            hop(d, b, own.at[b]).start()
    vouch(0)
    small[1].wait()
    small[2].wait()

    def wrapped(owner):
        return jnp.where(owner < 0, owner + nb, jnp.where(owner >= nb, owner - nb, owner))

    def found_in(ids, row, found):
        for s in range(SLOTS):
            entry = jnp.where(s < counts[0, row], lists[s, row], -1)
            found = jnp.where(ids == entry, 1, found)
        return found

    far = NB + 2 * near
    spot = lax.broadcasted_iota(jnp.int32, (mask.shape[1], E), 0)
    away = spot - NB
    second_half = away >= near
    dist = lax.shift_right_arithmetic(jnp.where(second_half, away - near, away), 2) + 1
    shift = jnp.where(second_half, dist, -dist)
    shift = jnp.where(spot >= far, jnp.where(spot >= far + NB, hops, -hops), shift)
    shift = jnp.where(spot < NB, 0, shift)
    ids = wrapped(me + shift) * NB + (spot & (NB - 1))
    founds = []
    for r in range(NB):
        found = found_in(ids, me * NB + r, jnp.zeros(ids.shape, jnp.int32))
        founds.append(found)
        mask[r, :, :] = found
    for d in range(2):
        rows = [[f[far + NB * d + c : far + NB * d + c + 1, :] for c in range(NB)] for f in founds]
        listed = [functools.reduce(jnp.maximum, [row[c] for row in rows]) for c in range(NB)]
        for at, chosen in enumerate(far_slots(listed)):
            for r in range(NB):
                live = sum(chosen[c] * rows[r][c] for c in range(NB))
                mask[r, far + 2 * d + at : far + 2 * d + at + 1, :] = live
    sub = lax.broadcasted_iota(jnp.int32, (8, E), 0)
    for d in range(2):
        toward = (right, left)[d]
        source = wrapped(me + (1 - hops, hops - 1)[d])
        blocks = source * NB + sub
        found = jnp.zeros((8, E), jnp.int32)
        for r in range(NB):
            found = found_in(blocks, toward * NB + r, found)
        for at, chosen in enumerate(far_slots([found[c : c + 1, :] for c in range(NB)])):
            for c in range(NB):
                pick[d, at, c, :, :] = chosen[c]

    acc[...] = jnp.zeros_like(acc)
    stage[...] = jnp.zeros_like(stage)
    tail = (lane < 3).astype(F32).astype(BF16)
    ones = jnp.ones((KP - K, BS), BF16)

    def block(slab, spot_index):
        keys = jnp.concatenate([slab[0:BS, :], tail], axis=1)
        panel = jnp.concatenate([slab[BS : BS + K, :], slab[BS + K : BS + 2 * K, :]], axis=1)
        panel = jnp.concatenate([panel, ones], axis=0)
        stats = slab[BS + 2 * K : ROWS, :].astype(F32)
        stats = jnp.concatenate([stats[0:8, :], stats[8:16, :]], axis=1)
        aq = 1.0 / stats[0:1, :]
        nq = stats[1:2, :] + stats[2:3, :] + stats[3:4, :]
        for r in range(NB):
            cross = nt_dot(xaug[r], keys)
            ap = apcol[r]
            power = ((cross - nq) * aq) * jnp.concatenate([ap, ap], axis=1)
            weights = jnp.exp2(power).astype(BF16)
            carried = nt_dot(panel, weights)
            live = mask[r, pl.ds(spot_index, 1), :]
            live = jnp.concatenate([live, live], axis=1)
            acc[r, :, :] += jnp.where(live > 0, carried, 0.0)

    def inside(b, carry):
        block(own.at[b], b)
        return carry

    lax.fori_loop(0, NB, inside, 0)

    def arrive(t, carry):
        last = t - (near - NB)
        for at in range(2):

            @pl.when(t == NB * (at + 1))
            def _():
                hear(at)
                vouch(at + 1)

        for d in range(2):
            hop(d, t, recv.at[d, t]).wait_recv()

            @pl.when(t < near - NB)
            def _():
                hop(d, t + NB, recv.at[d, t]).start()

            for at, (low, high) in enumerate(((0, 2), (1, 3))):

                @pl.when(jnp.logical_and(last >= low, last <= high))
                def _():
                    wanted = pick[d, at, last]
                    kept = stage[d, at].astype(F32)
                    taken = jnp.where(wanted > 0, recv[d, t].astype(F32), kept)
                    stage[d, at] = taken.astype(BF16)

                @pl.when(last == high)
                def _():
                    hop(d, near + at, stage.at[d, at]).start()

        for d in range(2):
            block(recv.at[d, t], NB + d * near + t)
        return carry

    lax.fori_loop(0, near, arrive, 0)
    hear(2)

    def arrive_far(t, carry):
        for d in range(2):
            hop(d, near + t, recv.at[d, near + t]).wait_recv()
        for d in range(2):
            block(recv.at[d, near + t], far + 2 * d + t)
        return carry

    lax.fori_loop(0, 2, arrive_far, 0)

    for r in range(NB):
        cols = slice(r * BS, (r + 1) * BS)
        total = acc[r, :, :]
        panel = jnp.concatenate([own[r, BS : BS + K, :], own[r, BS + K : BS + 2 * K, :]], axis=1)
        walked[:, cols] = (panel.astype(F32) + total[0:K, :]) / (1.0 + total[K : K + 1, :])
    flat = walked[...]
    gram = jnp.concatenate(
        [nt_dot(flat, flat, lax.Precision.HIGHEST), jnp.zeros((K, E - K), F32)], axis=1
    )

    def sent(t, carry):
        for d in range(2):
            hop(d, t, recv.at[d, t]).wait_send()
        return carry

    share = K // team

    def exchange(at, offsets, source, target, slot, peer):
        for o in offsets:
            pltpu.make_async_remote_copy(
                src_ref=source(o),
                dst_ref=target.at[slot],
                send_sem=asend.at[at],
                recv_sem=arecv.at[at],
                device_id=peer(o),
                device_id_type=MESH,
            ).start()

    def arrived(at, size, target):
        whole = target.at[pl.ds(0, size - 1)]
        return pltpu.make_async_remote_copy(
            src_ref=whole,
            dst_ref=whole,
            send_sem=asend.at[at],
            recv_sem=arecv.at[at],
            device_id=line_peer(1),
            device_id_type=MESH,
        )

    for i in range(team):
        g3[i] = gram[i * share : (i + 1) * share, :]
    exchange(0, team_offsets, lambda o: g3.at[team_peer(o)[1]], s0, rank, lambda o: team_peer(o)[0])
    s0[rank] = g3[rank]
    lax.fori_loop(0, steps, sent, 0)
    arrived(0, team, s0).wait_recv()
    p3[0] = jnp.sum(s0[...], axis=0)
    exchange(1, line_offsets, lambda o: p3.at[0], s1, zz, line_peer)
    s1[zz] = p3[0]
    arrived(1, nz, s1).wait_recv()
    p3[1] = jnp.sum(s1[...], axis=0)
    exchange(2, team_offsets, lambda o: p3.at[1], s2, rank, lambda o: team_peer(o)[0])
    s2[rank] = p3[1]
    arrived(2, team, s2).wait_recv()
    for i in range(team):
        gram_out[i * share : (i + 1) * share, :] = s2[i]
    arrived(0, team, s0).wait_send()
    arrived(1, nz, s1).wait_send()
    arrived(2, team, s2).wait_send()


def solve_kernel(root, gram, walked, ortho, r_factor):
    group = 8
    count = K // group
    sub = lax.broadcasted_iota(jnp.int32, (group, E), 0)
    col = lax.broadcasted_iota(jnp.int32, (group, E), 1)
    tiles = []
    for i in range(count):
        unit = (col == sub + (K + i * group)).astype(F32)
        tiles.append(gram[i * group : (i + 1) * group, :] + unit)
    for at in range(count):
        base = at * group
        wide = {
            i: [jnp.broadcast_to(tiles[i][:, base + k : base + k + 1], (group, E)) for k in range(group)]
            for i in range(at, count)
        }
        for k in range(group):
            inverse = 1.0 / wide[at][k][k : k + 1, :]
            row = tiles[at][k : k + 1, :] * inverse
            later = {m: wide[at][m][k : k + 1, :] * inverse for m in range(k + 1, group)}
            for i in range(at, count):
                factor = wide[i][k]
                if i == at:
                    factor = jnp.where(sub > k, factor, 0.0)
                tiles[i] = tiles[i] - factor * row
                for m, value in later.items():
                    wide[i][m] = wide[i][m] - factor * value
    rows = []
    for i in range(count):
        diagonal = jnp.sum(jnp.where(col == sub + i * group, tiles[i], 0.0), axis=1, keepdims=True)
        scaled = tiles[i] * (1.0 / jnp.sqrt(diagonal))
        upper = jnp.where(col >= sub + i * group, scaled, 0.0)
        r_factor[i * group : (i + 1) * group, :] = upper[:, 0:K] * (1.0 / root)
        rows.append(scaled[:, K : 2 * K] * root)
    ortho[0, :, :] = jnp.dot(
        jnp.concatenate(rows, axis=0),
        walked[...],
        precision=lax.Precision.HIGHEST,
        preferred_element_type=F32,
    )


def local(points, start_panel, seventh, neighbours, counts):
    nb = lax.axis_size("blk")
    ng = lax.axis_size("grp")
    nz = max(nb // 4, 1)
    hops = min(REACH, (nb - 1) // 2)
    pts = points.shape[1]
    team = (nb // nz) * ng
    share = K // team
    steps = NB * (hops - 1) + 2
    vmem = pl.BlockSpec(memory_space=pltpu.VMEM)
    hbm = pl.BlockSpec(memory_space=pltpu.HBM)
    walked, gram = pl.pallas_call(
        functools.partial(walk_kernel, (nb, ng, nz, hops)),
        out_shape=(
            jax.ShapeDtypeStruct((K, pts), F32),
            jax.ShapeDtypeStruct((K, E), F32),
        ),
        in_specs=[hbm] * 5,
        out_specs=(vmem, vmem),
        scratch_shapes=[
            pltpu.VMEM((1, pts), jnp.int32),
            pltpu.SMEM(neighbours.shape[:0:-1], jnp.int32),
            pltpu.SMEM(counts.shape, jnp.int32),
            pltpu.VMEM((NB, ROWS, E), BF16),
            pltpu.VMEM((2, steps, ROWS, E), BF16),
            pltpu.VMEM((2, 2, ROWS, E), BF16),
            pltpu.VMEM((NB, BS, 2 * E), BF16),
            pltpu.VMEM((NB, BS, E), F32),
            pltpu.VMEM((NB, KP, BS), F32),
            pltpu.VMEM((NB, 40, E), jnp.int32),
            pltpu.VMEM((2, 2, NB, 1, E), jnp.int32),
            pltpu.VMEM((team, share, E), F32),
            pltpu.VMEM((team, share, E), F32),
            pltpu.VMEM((nz, share, E), F32),
            pltpu.VMEM((team, share, E), F32),
            pltpu.VMEM((2, share, E), F32),
            pltpu.SemaphoreType.DMA((NB, 4)),
            pltpu.SemaphoreType.DMA((2, steps)),
            pltpu.SemaphoreType.DMA((2, steps)),
            pltpu.SemaphoreType.DMA((3,)),
            pltpu.SemaphoreType.DMA((3,)),
            pltpu.SemaphoreType.REGULAR((3,)),
        ],
        compiler_params=pltpu.CompilerParams(
            collective_id=0, has_side_effects=True, vmem_limit_bytes=32 * 1024 * 1024
        ),
        name="walk",
    )(
        *(
            pltpu.with_memory_space_constraint(each, pltpu.HBM)
            for each in (points, start_panel, seventh, jnp.swapaxes(neighbours, 1, 2), counts)
        )
    )
    root = math.sqrt(pts * nb * ng)
    return pl.pallas_call(
        functools.partial(solve_kernel, root),
        out_shape=(
            jax.ShapeDtypeStruct((1, K, pts), F32),
            jax.ShapeDtypeStruct((K, K), F32),
        ),
        in_specs=[vmem, vmem],
        out_specs=(vmem, vmem),
        compiler_params=pltpu.CompilerParams(vmem_limit_bytes=16 * 1024 * 1024),
        name="solve",
    )(gram, walked)


def solution(mesh):
    in_specs = (
        P("grp", "blk", None),
        P("grp", None, "blk"),
        P("grp", "blk"),
        P("grp", None, None),
        P("grp", None),
    )
    out_specs = (P("grp", None, "blk"), P())
    return jax.shard_map(local, mesh=mesh, in_specs=in_specs, out_specs=out_specs, check_vma=False)
```

```python
import functools
import math

import jax
import jax.numpy as jnp
from jax import lax
from jax.experimental import pallas as pl
from jax.experimental.pallas import tpu as pltpu
from jax.sharding import PartitionSpec as P

E = 128
K = 64
BS = 256
SLOTS = 16
NB = 4
ROWS = BS + 2 * K + 16
KP = K + 16
LOG2E = 1.4426950408889634
MESH = pl.DeviceIdType.MESH
F32 = jnp.float32
BF16 = jnp.bfloat16


def nt_dot(a, b, precision=None):
    return lax.dot_general(
        a, b, (((1,), (1,)), ((), ())), precision=precision, preferred_element_type=F32
    )


def split3(value):
    hi = value.astype(BF16).astype(F32)
    mid = (value - hi).astype(BF16).astype(F32)
    return hi, mid, value - hi - mid


def far_slots(listed):
    f0, f1, f2, f3 = listed
    n0, n1, n2, n3 = 1 - f0, 1 - f1, 1 - f2, 1 - f3
    first = (f0, n0 * f1, n0 * n1 * f2 * f3, jnp.zeros_like(f0))
    second = (jnp.zeros_like(f0), n3 * n2 * f1 * f0, n3 * f2, f3)
    return first, second


def walk_kernel(
    sizes, pts, pan, sev_in, lists_in, counts_in, walked, gram_out,
    sev, lists, counts, own, recv, stage, xaug, apcol, acc, mask, pick, rout, rin, g3, s0, s1, s2, p3,
    isem, ssem, rsem, osem, nsem, asend, arecv, heard,
):
    nb, ng, nz = sizes
    nx = nb // nz
    near = 2 * NB
    steps = near + 2
    me = lax.axis_index("blk")
    mg = lax.axis_index("grp")
    right = lax.rem(me + 1, nb)
    left = lax.rem(me + nb - 1, nb)
    zz = lax.rem(me, nz)
    xx = me // nz
    team = nx * ng
    rank = xx * ng + mg

    yy = mg // 2
    core = lax.rem(mg, 2)
    ny = ng // 2

    def team_peer(o):
        gx = lax.rem(xx + o[0], nx)
        gg = lax.rem(yy + o[1], ny) * 2 + lax.rem(core + o[2], 2)
        return (gx * nz + zz, gg), gx * ng + gg

    def line_peer(o):
        return (xx * nz + lax.rem(zz + o, nz), mg)

    def away_by(o, size):
        return min(o, size - o)

    team_offsets = [(a, b, c) for a in range(nx) for b in range(ny) for c in range(2)][1:]
    team_offsets.sort(key=lambda o: (-away_by(o[0], nx) - away_by(o[1], ny), o))
    line_offsets = sorted(range(1, nz), key=lambda o: (-away_by(o, nz), o))

    small = [
        pltpu.make_async_copy(sev_in, sev, isem.at[0, 3]),
        pltpu.make_async_copy(lists_in.at[0], lists, isem.at[1, 3]),
        pltpu.make_async_copy(counts_in, counts, isem.at[2, 3]),
    ]
    small[0].start()
    loads = []
    for b in range(NB):
        low = b * BS
        loads.append(
            [
                pltpu.make_async_copy(pts.at[0, low : low + BS, :], own.at[b, 0:BS, :], isem.at[b, 0]),
                pltpu.make_async_copy(
                    pan.at[0, :, low : low + E], own.at[b, BS : BS + K, :], isem.at[b, 1]
                ),
                pltpu.make_async_copy(
                    pan.at[0, :, low + E : low + BS], own.at[b, BS + K : BS + 2 * K, :], isem.at[b, 2]
                ),
            ]
        )
        for load in loads[b]:
            load.start()

    small[1].start()
    small[2].start()

    next_to = [line_peer(1), line_peer(nz - 1)]
    next_to += [team_peer(o)[0] for o in ((1, 0, 0), (nx - 1, 0, 0), (0, 1, 0), (0, ny - 1, 0), (0, 0, 1))]
    partners = [(right, mg), (left, mg)] + next_to
    rounds = [
        next_to,
        [line_peer(2), line_peer(nz - 2)]
        + [team_peer(o)[0] for o in ((2, 0, 0), (0, 2, 0), (1, 0, 0), (nx - 1, 0, 0))],
        [line_peer(4), line_peer(nz - 4), team_peer((0, 0, 1))[0]],
    ]

    def vouch(at):
        for partner in rounds[at]:
            pl.semaphore_signal(heard.at[at], inc=1, device_id=partner, device_id_type=MESH)

    def hear(at):
        pl.semaphore_wait(heard.at[at], len(rounds[at]))

    barrier = pltpu.get_barrier_semaphore()
    for partner in partners:
        pl.semaphore_signal(barrier, inc=1, device_id=partner, device_id_type=MESH)

    lane = lax.broadcasted_iota(jnp.int32, (BS, E), 1)

    def prepare(b):
        for load in loads[b]:
            load.wait()
        x = own[b, 0:BS, :]
        xf = x.astype(F32)
        place = jnp.broadcast_to(sev[0:1, b * BS : (b + 1) * BS].astype(F32), (E, BS)).T
        place = jnp.concatenate([place, place], axis=1).astype(jnp.int32)
        picked = (place == lax.broadcasted_iota(jnp.int32, (BS, BS), 1)).astype(F32).astype(BF16)
        partner = jnp.dot(picked, x, preferred_element_type=F32)
        diff = xf - partner
        scale = jnp.sqrt(jnp.sum(diff * diff, axis=1, keepdims=True) + 1e-06)
        scale = jnp.broadcast_to(scale, (BS, E)).astype(BF16).astype(F32)
        norm = jnp.broadcast_to(jnp.sum(xf * xf, axis=1, keepdims=True), (BS, E))
        hi, mid, low = split3(norm)
        zero = jnp.zeros_like(norm)
        columns = jnp.where(
            lane == 0, hi, jnp.where(lane == 1, mid, jnp.where(lane == 2, low, jnp.where(lane == 3, scale, zero)))
        )
        stats = columns.T[0:8, :]
        own[b, BS + 2 * K : ROWS, :] = jnp.concatenate([stats[:, :E], stats[:, E:]], axis=0).astype(BF16)
        keep_rows(0, b, xf, columns, scale)

    def keep_rows(who, b, xf, columns, scale):
        xaug[who, b, :, 0:E] = (2.0 * xf).astype(BF16)
        xaug[who, b, :, E : 2 * E] = jnp.where(lane < 3, -columns, 0.0).astype(BF16)
        apcol[who, b, :, :] = LOG2E / scale

    def row_stats(slab):
        stats = slab[BS + 2 * K : ROWS, :].astype(F32)
        return jnp.concatenate([stats[0:8, :], stats[8:16, :]], axis=1)

    def adopt(who, b, slab):
        columns = jnp.concatenate([row_stats(slab)] * (E // 8), axis=0).T
        keep_rows(who, b, slab[0:BS, :].astype(F32), columns, jnp.broadcast_to(columns[:, 3:4], (BS, E)))

    def hop(d, slot, source):
        return pltpu.make_async_remote_copy(
            src_ref=source,
            dst_ref=recv.at[d, slot],
            send_sem=ssem.at[d, slot],
            recv_sem=rsem.at[d, slot],
            device_id=((right, left)[d], mg),
            device_id_type=MESH,
        )

    small[0].wait()
    prepare(0)
    pl.semaphore_wait(barrier, len(partners))
    for b in range(NB):
        if b:
            prepare(b)
        for d in range(2):
            hop(d, b, own.at[b]).start()
    vouch(0)
    small[1].wait()
    small[2].wait()

    def wrapped(owner):
        return jnp.where(owner < 0, owner + nb, jnp.where(owner >= nb, owner - nb, owner))

    def found_in(ids, row, found):
        for s in range(SLOTS):
            entry = jnp.where(s < counts[0, row], lists[s, row], -1)
            found = jnp.where(ids == entry, 1, found)
        return found

    spot = lax.broadcasted_iota(jnp.int32, (mask.shape[2], E), 0)
    away = spot - NB
    dist = lax.shift_right_arithmetic(jnp.where(away >= near, away - near, away), 2) + 1
    shift = jnp.where(spot < NB, 0, jnp.where(away >= near, dist, -dist))
    ids = wrapped(me + shift) * NB + (spot & (NB - 1))
    for r in range(NB):
        mask[0, r, :, :] = found_in(ids, me * NB + r, jnp.zeros(ids.shape, jnp.int32))
    sub = lax.broadcasted_iota(jnp.int32, (8, E), 0)
    for d in range(2):
        toward = (right, left)[d]
        side = 2 * d - 1
        ids = wrapped(me + jnp.where(sub < NB, 2 * side, 3 * side)) * NB + (sub & (NB - 1))
        founds = [found_in(ids, toward * NB + r, jnp.zeros((8, E), jnp.int32)) for r in range(NB)]
        rows = [[f[NB + c : NB + c + 1, :] for c in range(NB)] for f in founds]
        listed = [functools.reduce(jnp.maximum, [row[c] for row in rows]) for c in range(NB)]
        for r in range(NB):
            mask[1 + d, r, 0:8, :] = founds[r]
            for at, chosen in enumerate(far_slots(listed)):
                mask[1 + d, r, NB + at : NB + at + 1, :] = sum(chosen[c] * rows[r][c] for c in range(NB))
        blocks = wrapped(me + 2 * side) * NB + sub
        found = jnp.zeros((8, E), jnp.int32)
        for r in range(NB):
            found = found_in(blocks, wrapped(me - 2 * side) * NB + r, found)
        for at, chosen in enumerate(far_slots([found[c : c + 1, :] for c in range(NB)])):
            for c in range(NB):
                pick[d, at, c, :, :] = chosen[c]

    acc[...] = jnp.zeros_like(acc)
    stage[...] = jnp.zeros_like(stage)
    tail = (lane < 3).astype(F32).astype(BF16)
    ones = jnp.ones((KP - K, BS), BF16)

    def block(slab, who, spot_index):
        keys = jnp.concatenate([slab[0:BS, :], tail], axis=1)
        panel = jnp.concatenate([slab[BS : BS + K, :], slab[BS + K : BS + 2 * K, :]], axis=1)
        panel = jnp.concatenate([panel, ones], axis=0)
        stats = row_stats(slab)
        aq = 1.0 / stats[3:4, :]
        nq = stats[0:1, :] + stats[1:2, :] + stats[2:3, :]
        for r in range(NB):
            cross = nt_dot(xaug[who, r], keys)
            ap = apcol[who, r]
            power = ((cross - nq) * aq) * jnp.concatenate([ap, ap], axis=1)
            weights = jnp.exp2(power).astype(BF16)
            carried = nt_dot(panel, weights)
            live = mask[who, r, pl.ds(spot_index, 1), :]
            live = jnp.concatenate([live, live], axis=1)
            acc[who, r, :, :] += jnp.where(live > 0, carried, 0.0)

    def inside(b, carry):
        block(own.at[b], 0, b)
        return carry

    lax.fori_loop(0, NB, inside, 0)

    def first_hop(t, carry):
        for d in range(2):
            hop(d, t, recv.at[d, t]).wait_recv()
            hop(d, t + NB, recv.at[d, t]).start()

        @pl.when(t == NB - 1)
        def _():
            hear(0)
            vouch(1)

        for d in range(2):
            block(recv.at[d, t], 0, NB + d * near + t)
            adopt(2 - d, t, recv.at[d, t])
        return carry

    lax.fori_loop(0, NB, first_hop, 0)

    def second_hop(c, carry):
        t = c + NB
        for d in range(2):
            hop(d, t, recv.at[d, t]).wait_recv()
            for at, (low, high) in enumerate(((0, 2), (1, 3))):

                @pl.when(jnp.logical_and(c >= low, c <= high))
                def _():
                    wanted = pick[d, at, c]
                    kept = stage[d, at].astype(F32)
                    taken = jnp.where(wanted > 0, recv[d, t].astype(F32), kept)
                    stage[d, at] = taken.astype(BF16)

                @pl.when(c == high)
                def _():
                    hop(d, near + at, stage.at[d, at]).start()

        @pl.when(c == 2)
        def _():
            hear(1)
            vouch(2)

        for d in range(2):
            block(recv.at[d, t], 1 + d, c)
        return carry

    lax.fori_loop(0, NB, second_hop, 0)

    def third_hop(at, carry):
        for d in range(2):
            hop(d, near + at, recv.at[d, near + at]).wait_recv()
        for d in range(2):
            block(recv.at[d, near + at], 1 + d, NB + at)
        return carry

    lax.fori_loop(0, 2, third_hop, 0)

    def result(d, r):
        return pltpu.make_async_remote_copy(
            src_ref=rout.at[d, r],
            dst_ref=rin.at[d, r],
            send_sem=osem.at[d, r],
            recv_sem=nsem.at[d, r],
            device_id=((right, left)[d], mg),
            device_id_type=MESH,
        )

    rest = lax.broadcasted_iota(jnp.int32, (KP - K, BS), 0)
    for r in range(NB):
        for d in range(2):
            degree = acc[1 + d, r, K:KP, :]
            high = degree.astype(BF16).astype(F32)
            degree = jnp.where(rest == 0, high, jnp.where(rest == 1, degree - high, 0.0))
            rout[d, r, 0:K, :] = acc[1 + d, r, 0:K, :].astype(BF16)
            rout[d, r, K:KP, :] = degree.astype(BF16)
            result(d, r).start()

    def own_rows_later(t, carry):
        for d in range(2):
            block(recv.at[d, t], 0, NB + d * near + t)
        return carry

    lax.fori_loop(NB, near, own_rows_later, 0)
    hear(2)

    for r in range(NB):
        cols = slice(r * BS, (r + 1) * BS)
        total = acc[0, r, 0 : K + 8, :]
        for d in range(2):
            result(d, r).wait_recv()
            more = rin[d, r, :, :].astype(F32)
            extra = more[K : K + 1, :] + more[K + 1 : K + 2, :]
            total = total + jnp.concatenate([more[0:K, :], jnp.broadcast_to(extra, (8, BS))], axis=0)
        panel = jnp.concatenate([own[r, BS : BS + K, :], own[r, BS + K : BS + 2 * K, :]], axis=1)
        walked[:, cols] = (panel.astype(F32) + total[0:K, :]) / (1.0 + total[K : K + 1, :])
    flat = walked[...]
    gram = jnp.concatenate(
        [nt_dot(flat, flat, lax.Precision.HIGHEST), jnp.zeros((K, E - K), F32)], axis=1
    )

    def sent(t, carry):
        for d in range(2):
            hop(d, t, recv.at[d, t]).wait_send()
        return carry

    for d in range(2):
        for r in range(NB):
            result(d, r).wait_send()

    share = K // team

    def exchange(at, offsets, source, target, slot, peer):
        for o in offsets:
            pltpu.make_async_remote_copy(
                src_ref=source(o),
                dst_ref=target.at[slot],
                send_sem=asend.at[at],
                recv_sem=arecv.at[at],
                device_id=peer(o),
                device_id_type=MESH,
            ).start()

    def arrived(at, size, target):
        whole = target.at[pl.ds(0, size - 1)]
        return pltpu.make_async_remote_copy(
            src_ref=whole,
            dst_ref=whole,
            send_sem=asend.at[at],
            recv_sem=arecv.at[at],
            device_id=line_peer(1),
            device_id_type=MESH,
        )

    for i in range(team):
        g3[i] = gram[i * share : (i + 1) * share, :]
    exchange(0, team_offsets, lambda o: g3.at[team_peer(o)[1]], s0, rank, lambda o: team_peer(o)[0])
    s0[rank] = g3[rank]
    lax.fori_loop(0, steps, sent, 0)
    arrived(0, team, s0).wait_recv()
    p3[0] = jnp.sum(s0[...], axis=0)
    exchange(1, line_offsets, lambda o: p3.at[0], s1, zz, line_peer)
    s1[zz] = p3[0]
    arrived(1, nz, s1).wait_recv()
    p3[1] = jnp.sum(s1[...], axis=0)
    exchange(2, team_offsets, lambda o: p3.at[1], s2, rank, lambda o: team_peer(o)[0])
    s2[rank] = p3[1]
    arrived(2, team, s2).wait_recv()
    for i in range(team):
        gram_out[i * share : (i + 1) * share, :] = s2[i]
    arrived(0, team, s0).wait_send()
    arrived(1, nz, s1).wait_send()
    arrived(2, team, s2).wait_send()


def solve_kernel(root, gram, walked, ortho, r_factor):
    group = 8
    count = K // group
    sub = lax.broadcasted_iota(jnp.int32, (group, E), 0)
    col = lax.broadcasted_iota(jnp.int32, (group, E), 1)
    tiles = []
    for i in range(count):
        unit = (col == sub + (K + i * group)).astype(F32)
        tiles.append(gram[i * group : (i + 1) * group, :] + unit)
    for at in range(count):
        base = at * group
        wide = {
            i: [jnp.broadcast_to(tiles[i][:, base + k : base + k + 1], (group, E)) for k in range(group)]
            for i in range(at, count)
        }
        for k in range(group):
            inverse = 1.0 / wide[at][k][k : k + 1, :]
            row = tiles[at][k : k + 1, :] * inverse
            later = {m: wide[at][m][k : k + 1, :] * inverse for m in range(k + 1, group)}
            for i in range(at, count):
                factor = wide[i][k]
                if i == at:
                    factor = jnp.where(sub > k, factor, 0.0)
                tiles[i] = tiles[i] - factor * row
                for m, value in later.items():
                    wide[i][m] = wide[i][m] - factor * value
    rows = []
    for i in range(count):
        diagonal = jnp.sum(jnp.where(col == sub + i * group, tiles[i], 0.0), axis=1, keepdims=True)
        scaled = tiles[i] * (1.0 / jnp.sqrt(diagonal))
        upper = jnp.where(col >= sub + i * group, scaled, 0.0)
        r_factor[i * group : (i + 1) * group, :] = upper[:, 0:K] * (1.0 / root)
        rows.append(scaled[:, K : 2 * K] * root)
    ortho[0, :, :] = jnp.dot(
        jnp.concatenate(rows, axis=0),
        walked[...],
        precision=lax.Precision.HIGHEST,
        preferred_element_type=F32,
    )


def local(points, start_panel, seventh, neighbours, counts):
    nb = lax.axis_size("blk")
    ng = lax.axis_size("grp")
    nz = max(nb // 4, 1)
    pts = points.shape[1]
    team = (nb // nz) * ng
    share = K // team
    steps = 2 * NB + 2
    vmem = pl.BlockSpec(memory_space=pltpu.VMEM)
    hbm = pl.BlockSpec(memory_space=pltpu.HBM)
    walked, gram = pl.pallas_call(
        functools.partial(walk_kernel, (nb, ng, nz)),
        out_shape=(
            jax.ShapeDtypeStruct((K, pts), F32),
            jax.ShapeDtypeStruct((K, E), F32),
        ),
        in_specs=[hbm] * 5,
        out_specs=(vmem, vmem),
        scratch_shapes=[
            pltpu.VMEM((1, pts), jnp.int32),
            pltpu.SMEM(neighbours.shape[:0:-1], jnp.int32),
            pltpu.SMEM(counts.shape, jnp.int32),
            pltpu.VMEM((NB, ROWS, E), BF16),
            pltpu.VMEM((2, steps, ROWS, E), BF16),
            pltpu.VMEM((2, 2, ROWS, E), BF16),
            pltpu.VMEM((3, NB, BS, 2 * E), BF16),
            pltpu.VMEM((3, NB, BS, E), F32),
            pltpu.VMEM((3, NB, KP, BS), F32),
            pltpu.VMEM((3, NB, 24, E), jnp.int32),
            pltpu.VMEM((2, 2, NB, 1, E), jnp.int32),
            pltpu.VMEM((2, NB, KP, BS), BF16),
            pltpu.VMEM((2, NB, KP, BS), BF16),
            pltpu.VMEM((team, share, E), F32),
            pltpu.VMEM((team, share, E), F32),
            pltpu.VMEM((nz, share, E), F32),
            pltpu.VMEM((team, share, E), F32),
            pltpu.VMEM((2, share, E), F32),
            pltpu.SemaphoreType.DMA((NB, 4)),
            pltpu.SemaphoreType.DMA((2, steps)),
            pltpu.SemaphoreType.DMA((2, steps)),
            pltpu.SemaphoreType.DMA((2, NB)),
            pltpu.SemaphoreType.DMA((2, NB)),
            pltpu.SemaphoreType.DMA((3,)),
            pltpu.SemaphoreType.DMA((3,)),
            pltpu.SemaphoreType.REGULAR((3,)),
        ],
        compiler_params=pltpu.CompilerParams(
            collective_id=0, has_side_effects=True, vmem_limit_bytes=32 * 1024 * 1024
        ),
        name="walk",
    )(
        *(
            pltpu.with_memory_space_constraint(each, pltpu.HBM)
            for each in (points, start_panel, seventh, jnp.swapaxes(neighbours, 1, 2), counts)
        )
    )
    root = math.sqrt(pts * nb * ng)
    return pl.pallas_call(
        functools.partial(solve_kernel, root),
        out_shape=(
            jax.ShapeDtypeStruct((1, K, pts), F32),
            jax.ShapeDtypeStruct((K, K), F32),
        ),
        in_specs=[vmem, vmem],
        out_specs=(vmem, vmem),
        compiler_params=pltpu.CompilerParams(vmem_limit_bytes=16 * 1024 * 1024),
        name="solve",
    )(gram, walked)


def solution(mesh):
    in_specs = (
        P("grp", "blk", None),
        P("grp", None, "blk"),
        P("grp", "blk"),
        P("grp", None, None),
        P("grp", None),
    )
    out_specs = (P("grp", None, "blk"), P())
    return jax.shard_map(local, mesh=mesh, in_specs=in_specs, out_specs=out_specs, check_vma=False)
```

```python
import functools
import math

import jax
import jax.numpy as jnp
from jax import lax
from jax.experimental import pallas as pl
from jax.experimental.pallas import tpu as pltpu
from jax.sharding import PartitionSpec as P

E = 128
K = 64
BS = 256
SLOTS = 16
NB = 4
ROWS = BS + 2 * K + 8
KP = K + 8
LOG2E = 1.4426950408889634
MESH = pl.DeviceIdType.MESH
F32 = jnp.float32
BF16 = jnp.bfloat16


def nt_dot(a, b, precision=None):
    return lax.dot_general(
        a, b, (((1,), (1,)), ((), ())), precision=precision, preferred_element_type=F32
    )


def split3(value):
    hi = value.astype(BF16).astype(F32)
    mid = (value - hi).astype(BF16).astype(F32)
    return hi, mid, value - hi - mid


def far_slots(listed):
    f0, f1, f2, f3 = listed
    n0, n1, n2, n3 = 1 - f0, 1 - f1, 1 - f2, 1 - f3
    first = (f0, n0 * f1, n0 * n1 * f2 * f3, jnp.zeros_like(f0))
    second = (jnp.zeros_like(f0), n3 * n2 * f1 * f0, n3 * f2, f3)
    return first, second


def walk_kernel(
    sizes, pts, pan, sev_in, lists_in, counts_in, walked, gram_out,
    sev, lists, counts, own, recv, stage, xaug, apcol, acc, mask, pick, rout, rin, g3, s0, s1, s2, p3,
    isem, ssem, rsem, osem, nsem, asend, arecv, heard,
):
    nb, ng, nz = sizes
    nx = nb // nz
    near = 2 * NB
    steps = near + 2
    me = lax.axis_index("blk")
    mg = lax.axis_index("grp")
    right = lax.rem(me + 1, nb)
    left = lax.rem(me + nb - 1, nb)
    zz = lax.rem(me, nz)
    xx = me // nz
    team = nx * ng
    rank = xx * ng + mg

    yy = mg // 2
    core = lax.rem(mg, 2)
    ny = ng // 2

    def team_peer(o):
        gx = lax.rem(xx + o[0], nx)
        gg = lax.rem(yy + o[1], ny) * 2 + lax.rem(core + o[2], 2)
        return (gx * nz + zz, gg), gx * ng + gg

    def line_peer(o):
        return (xx * nz + lax.rem(zz + o, nz), mg)

    def away_by(o, size):
        return min(o, size - o)

    team_offsets = [(a, b, c) for a in range(nx) for b in range(ny) for c in range(2)][1:]
    team_offsets.sort(key=lambda o: (-away_by(o[0], nx) - away_by(o[1], ny), o))
    line_offsets = sorted(range(1, nz), key=lambda o: (-away_by(o, nz), o))

    small = [
        pltpu.make_async_copy(sev_in, sev, isem.at[0, 3]),
        pltpu.make_async_copy(lists_in.at[0], lists, isem.at[1, 3]),
        pltpu.make_async_copy(counts_in, counts, isem.at[2, 3]),
    ]
    small[0].start()
    loads = []
    for b in range(NB):
        low = b * BS
        loads.append(
            [
                pltpu.make_async_copy(pts.at[0, low : low + BS, :], own.at[b, 0:BS, :], isem.at[b, 0]),
                pltpu.make_async_copy(
                    pan.at[0, :, low : low + E], own.at[b, BS : BS + K, :], isem.at[b, 1]
                ),
                pltpu.make_async_copy(
                    pan.at[0, :, low + E : low + BS], own.at[b, BS + K : BS + 2 * K, :], isem.at[b, 2]
                ),
            ]
        )
        for load in loads[b]:
            load.start()

    small[1].start()
    small[2].start()

    next_to = [line_peer(1), line_peer(nz - 1)]
    next_to += [team_peer(o)[0] for o in ((1, 0, 0), (nx - 1, 0, 0), (0, 1, 0), (0, ny - 1, 0), (0, 0, 1))]
    partners = [(right, mg), (left, mg)] + next_to
    rounds = [
        next_to,
        [line_peer(2), line_peer(nz - 2)]
        + [team_peer(o)[0] for o in ((2, 0, 0), (0, 2, 0), (1, 0, 0), (nx - 1, 0, 0))],
        [line_peer(4), line_peer(nz - 4), team_peer((0, 0, 1))[0]],
    ]

    def vouch(at):
        for partner in rounds[at]:
            pl.semaphore_signal(heard.at[at], inc=1, device_id=partner, device_id_type=MESH)

    def hear(at):
        pl.semaphore_wait(heard.at[at], len(rounds[at]))

    barrier = pltpu.get_barrier_semaphore()
    for partner in partners:
        pl.semaphore_signal(barrier, inc=1, device_id=partner, device_id_type=MESH)

    lane = lax.broadcasted_iota(jnp.int32, (BS, E), 1)

    def prepare(b):
        for load in loads[b]:
            load.wait()
        x = own[b, 0:BS, :]
        xf = x.astype(F32)
        place = jnp.broadcast_to(sev[0:1, b * BS : (b + 1) * BS].astype(F32), (E, BS)).T
        place = jnp.concatenate([place, place], axis=1).astype(jnp.int32)
        picked = (place == lax.broadcasted_iota(jnp.int32, (BS, BS), 1)).astype(F32).astype(BF16)
        partner = jnp.dot(picked, x, preferred_element_type=F32)
        diff = xf - partner
        scale = jnp.sqrt(jnp.sum(diff * diff, axis=1, keepdims=True) + 1e-06)
        scale = jnp.broadcast_to(scale, (BS, E)).astype(BF16).astype(F32)
        norm = jnp.broadcast_to(jnp.sum(xf * xf, axis=1, keepdims=True), (BS, E))
        hi, mid, low = split3(norm)
        zero = jnp.zeros_like(norm)
        columns = jnp.where(
            lane == 0, hi, jnp.where(lane == 1, mid, jnp.where(lane == 2, low, jnp.where(lane == 3, scale, zero)))
        )
        stats = columns.T[0:4, :]
        own[b, BS + 2 * K : ROWS, :] = jnp.concatenate([stats[:, :E], stats[:, E:]], axis=0).astype(BF16)
        keep_rows(0, b, xf, columns, scale)

    def keep_rows(who, b, xf, columns, scale):
        xaug[who, b, :, 0:E] = (2.0 * xf).astype(BF16)
        xaug[who, b, :, E : 2 * E] = jnp.where(lane < 3, -columns, 0.0).astype(BF16)
        apcol[who, b, :, :] = LOG2E / scale

    def row_stats(slab):
        stats = slab[BS + 2 * K : ROWS, :].astype(F32)
        return jnp.concatenate([stats[0:4, :], stats[4:8, :]], axis=1)

    def adopt(who, b, slab):
        columns = jnp.concatenate([row_stats(slab)] * (E // 4), axis=0).T
        keep_rows(who, b, slab[0:BS, :].astype(F32), columns, jnp.broadcast_to(columns[:, 3:4], (BS, E)))

    def hop(d, slot, source):
        return pltpu.make_async_remote_copy(
            src_ref=source,
            dst_ref=recv.at[d, slot],
            send_sem=ssem.at[d, slot],
            recv_sem=rsem.at[d, slot],
            device_id=((right, left)[d], mg),
            device_id_type=MESH,
        )

    small[0].wait()
    prepare(0)
    pl.semaphore_wait(barrier, len(partners))
    for b in range(NB):
        if b:
            prepare(b)
        for d in range(2):
            hop(d, b, own.at[b]).start()
    vouch(0)
    small[1].wait()
    small[2].wait()

    def wrapped(owner):
        return jnp.where(owner < 0, owner + nb, jnp.where(owner >= nb, owner - nb, owner))

    def found_in(ids, row, found):
        for s in range(SLOTS):
            entry = jnp.where(s < counts[0, row], lists[s, row], -1)
            found = jnp.where(ids == entry, 1, found)
        return found

    spot = lax.broadcasted_iota(jnp.int32, (mask.shape[2], E), 0)
    away = spot - NB
    dist = lax.shift_right_arithmetic(jnp.where(away >= near, away - near, away), 2) + 1
    shift = jnp.where(spot < NB, 0, jnp.where(away >= near, dist, -dist))
    ids = wrapped(me + shift) * NB + (spot & (NB - 1))
    for r in range(NB):
        mask[0, r, :, :] = found_in(ids, me * NB + r, jnp.zeros(ids.shape, jnp.int32))
    sub = lax.broadcasted_iota(jnp.int32, (8, E), 0)
    for d in range(2):
        toward = (right, left)[d]
        side = 2 * d - 1
        ids = wrapped(me + jnp.where(sub < NB, 2 * side, 3 * side)) * NB + (sub & (NB - 1))
        founds = [found_in(ids, toward * NB + r, jnp.zeros((8, E), jnp.int32)) for r in range(NB)]
        rows = [[f[NB + c : NB + c + 1, :] for c in range(NB)] for f in founds]
        listed = [functools.reduce(jnp.maximum, [row[c] for row in rows]) for c in range(NB)]
        for r in range(NB):
            mask[1 + d, r, 0:8, :] = founds[r]
            for at, chosen in enumerate(far_slots(listed)):
                mask[1 + d, r, NB + at : NB + at + 1, :] = sum(chosen[c] * rows[r][c] for c in range(NB))
        blocks = wrapped(me + 2 * side) * NB + sub
        found = jnp.zeros((8, E), jnp.int32)
        for r in range(NB):
            found = found_in(blocks, wrapped(me - 2 * side) * NB + r, found)
        for at, chosen in enumerate(far_slots([found[c : c + 1, :] for c in range(NB)])):
            for c in range(NB):
                pick[d, at, c, :, :] = chosen[c]

    acc[...] = jnp.zeros_like(acc)
    stage[...] = jnp.zeros_like(stage)
    tail = (lane < 3).astype(F32).astype(BF16)
    ones = jnp.ones((KP - K, BS), BF16)

    def block(slab, who, spot_index):
        keys = jnp.concatenate([slab[0:BS, :], tail], axis=1)
        panel = jnp.concatenate([slab[BS : BS + K, :], slab[BS + K : BS + 2 * K, :]], axis=1)
        panel = jnp.concatenate([panel, ones], axis=0)
        stats = row_stats(slab)
        aq = 1.0 / stats[3:4, :]
        nq = stats[0:1, :] + stats[1:2, :] + stats[2:3, :]
        for r in range(NB):
            cross = nt_dot(xaug[who, r], keys)
            ap = apcol[who, r]
            power = ((cross - nq) * aq) * jnp.concatenate([ap, ap], axis=1)
            weights = jnp.exp2(power).astype(BF16)
            carried = nt_dot(panel, weights)
            live = mask[who, r, pl.ds(spot_index, 1), :]
            live = jnp.concatenate([live, live], axis=1)
            acc[who, r, :, :] += jnp.where(live > 0, carried, 0.0)

    def inside(b, carry):
        block(own.at[b], 0, b)
        return carry

    lax.fori_loop(0, NB, inside, 0)

    def first_hop(t, carry):
        for d in range(2):
            hop(d, t, recv.at[d, t]).wait_recv()
            hop(d, t + NB, recv.at[d, t]).start()

        @pl.when(t == NB - 1)
        def _():
            hear(0)
            vouch(1)

        for d in range(2):
            block(recv.at[d, t], 0, NB + d * near + t)
            adopt(2 - d, t, recv.at[d, t])
        return carry

    lax.fori_loop(0, NB, first_hop, 0)

    def second_hop(c, carry):
        t = c + NB
        for d in range(2):
            hop(d, t, recv.at[d, t]).wait_recv()
            for at, (low, high) in enumerate(((0, 2), (1, 3))):

                @pl.when(jnp.logical_and(c >= low, c <= high))
                def _():
                    wanted = pick[d, at, c]
                    kept = stage[d, at].astype(F32)
                    taken = jnp.where(wanted > 0, recv[d, t].astype(F32), kept)
                    stage[d, at] = taken.astype(BF16)

                @pl.when(c == high)
                def _():
                    hop(d, near + at, stage.at[d, at]).start()

        @pl.when(c == 2)
        def _():
            hear(1)
            vouch(2)

        for d in range(2):
            block(recv.at[d, t], 1 + d, c)
        return carry

    lax.fori_loop(0, NB, second_hop, 0)

    def third_hop(at, carry):
        for d in range(2):
            hop(d, near + at, recv.at[d, near + at]).wait_recv()
        for d in range(2):
            block(recv.at[d, near + at], 1 + d, NB + at)
        return carry

    lax.fori_loop(0, 2, third_hop, 0)

    def result(d, r):
        return pltpu.make_async_remote_copy(
            src_ref=rout.at[d, r],
            dst_ref=rin.at[d, r],
            send_sem=osem.at[d, r],
            recv_sem=nsem.at[d, r],
            device_id=((right, left)[d], mg),
            device_id_type=MESH,
        )

    rest = lax.broadcasted_iota(jnp.int32, (KP - K, BS), 0)
    for r in range(NB):
        for d in range(2):
            degree = acc[1 + d, r, K:KP, :]
            high = degree.astype(BF16).astype(F32)
            degree = jnp.where(rest == 0, high, jnp.where(rest == 1, degree - high, 0.0))
            rout[d, r, 0:K, :] = acc[1 + d, r, 0:K, :].astype(BF16)
            rout[d, r, K:KP, :] = degree.astype(BF16)
            result(d, r).start()

    def own_rows_later(t, carry):
        for d in range(2):
            block(recv.at[d, t], 0, NB + d * near + t)
        return carry

    lax.fori_loop(NB, near, own_rows_later, 0)
    hear(2)

    for r in range(NB):
        cols = slice(r * BS, (r + 1) * BS)
        total = acc[0, r, 0 : K + 8, :]
        for d in range(2):
            result(d, r).wait_recv()
            more = rin[d, r, :, :].astype(F32)
            extra = more[K : K + 1, :] + more[K + 1 : K + 2, :]
            total = total + jnp.concatenate([more[0:K, :], jnp.broadcast_to(extra, (8, BS))], axis=0)
        panel = jnp.concatenate([own[r, BS : BS + K, :], own[r, BS + K : BS + 2 * K, :]], axis=1)
        walked[:, cols] = (panel.astype(F32) + total[0:K, :]) / (1.0 + total[K : K + 1, :])
    flat = walked[...]
    gram = nt_dot(flat, jnp.concatenate([flat, flat], axis=0), lax.Precision.HIGHEST)
    half = lax.broadcasted_iota(jnp.int32, (K // 2, E), 1) < K
    packed = jnp.where(half, gram[0 : K // 2, :], gram[K // 2 : K, :])

    def sent(t, carry):
        for d in range(2):
            hop(d, t, recv.at[d, t]).wait_send()
        return carry

    for d in range(2):
        for r in range(NB):
            result(d, r).wait_send()

    share = K // 2 // ng
    grp_offsets = [o for o in team_offsets if o[0] == 0]

    def exchange(at, offsets, source, target, slot, peer):
        for o in offsets:
            pltpu.make_async_remote_copy(
                src_ref=source(o),
                dst_ref=target.at[slot],
                send_sem=asend.at[at],
                recv_sem=arecv.at[at],
                device_id=peer(o),
                device_id_type=MESH,
            ).start()

    def arrived(at, size, target):
        whole = target.at[pl.ds(0, size - 1)]
        return pltpu.make_async_remote_copy(
            src_ref=whole,
            dst_ref=whole,
            send_sem=asend.at[at],
            recv_sem=arecv.at[at],
            device_id=line_peer(1),
            device_id_type=MESH,
        )

    for i in range(ng):
        g3[i] = packed[i * share : (i + 1) * share, :]
    exchange(
        0, grp_offsets, lambda o: g3.at[team_peer(o)[0][1]], s0, mg, lambda o: team_peer(o)[0]
    )
    s0[mg] = g3[mg]
    lax.fori_loop(0, steps, sent, 0)
    arrived(0, ng, s0).wait_recv()
    p3[0] = jnp.sum(s0[...], axis=0)
    exchange(1, line_offsets, lambda o: p3.at[0], s1, zz, line_peer)
    s1[zz] = p3[0]
    arrived(1, nz, s1).wait_recv()
    p3[1] = jnp.sum(s1[...], axis=0)
    exchange(2, team_offsets, lambda o: p3.at[1], s2, rank, lambda o: team_peer(o)[0])
    s2[rank] = p3[1]
    arrived(2, team, s2).wait_recv()
    whole = []
    for i in range(ng):
        part = s2[i]
        for x in range(1, nx):
            part = part + s2[x * ng + i]
        whole.append(part)
    whole = jnp.concatenate(whole, axis=0)
    gram_out[0 : K // 2, :] = jnp.where(half, whole, 0.0)
    gram_out[K // 2 : K, :] = jnp.where(half, pltpu.roll(whole, K, 1), 0.0)
    arrived(0, ng, s0).wait_send()
    arrived(1, nz, s1).wait_send()
    arrived(2, team, s2).wait_send()


def solve_kernel(root, gram, walked, ortho, r_factor):
    group = 8
    count = K // group
    sub = lax.broadcasted_iota(jnp.int32, (group, E), 0)
    col = lax.broadcasted_iota(jnp.int32, (group, E), 1)
    tiles = []
    for i in range(count):
        unit = (col == sub + (K + i * group)).astype(F32)
        tiles.append(gram[i * group : (i + 1) * group, :] + unit)
    for at in range(count):
        base = at * group
        wide = {
            i: [jnp.broadcast_to(tiles[i][:, base + k : base + k + 1], (group, E)) for k in range(group)]
            for i in range(at, count)
        }
        for k in range(group):
            inverse = 1.0 / wide[at][k][k : k + 1, :]
            row = tiles[at][k : k + 1, :] * inverse
            later = {m: wide[at][m][k : k + 1, :] * inverse for m in range(k + 1, group)}
            for i in range(at, count):
                factor = wide[i][k]
                if i == at:
                    factor = jnp.where(sub > k, factor, 0.0)
                tiles[i] = tiles[i] - factor * row
                for m, value in later.items():
                    wide[i][m] = wide[i][m] - factor * value
    rows = []
    for i in range(count):
        diagonal = jnp.sum(jnp.where(col == sub + i * group, tiles[i], 0.0), axis=1, keepdims=True)
        scaled = tiles[i] * (1.0 / jnp.sqrt(diagonal))
        upper = jnp.where(col >= sub + i * group, scaled, 0.0)
        r_factor[i * group : (i + 1) * group, :] = upper[:, 0:K] * (1.0 / root)
        rows.append(scaled[:, K : 2 * K] * root)
    ortho[0, :, :] = jnp.dot(
        jnp.concatenate(rows, axis=0),
        walked[...],
        precision=lax.Precision.HIGHEST,
        preferred_element_type=F32,
    )


def local(points, start_panel, seventh, neighbours, counts):
    nb = lax.axis_size("blk")
    ng = lax.axis_size("grp")
    nz = max(nb // 4, 1)
    pts = points.shape[1]
    team = (nb // nz) * ng
    share = K // 2 // ng
    steps = 2 * NB + 2
    vmem = pl.BlockSpec(memory_space=pltpu.VMEM)
    hbm = pl.BlockSpec(memory_space=pltpu.HBM)
    walked, gram = pl.pallas_call(
        functools.partial(walk_kernel, (nb, ng, nz)),
        out_shape=(
            jax.ShapeDtypeStruct((K, pts), F32),
            jax.ShapeDtypeStruct((K, E), F32),
        ),
        in_specs=[hbm] * 5,
        out_specs=(vmem, vmem),
        scratch_shapes=[
            pltpu.VMEM((1, pts), jnp.int32),
            pltpu.SMEM(neighbours.shape[:0:-1], jnp.int32),
            pltpu.SMEM(counts.shape, jnp.int32),
            pltpu.VMEM((NB, ROWS, E), BF16),
            pltpu.VMEM((2, steps, ROWS, E), BF16),
            pltpu.VMEM((2, 2, ROWS, E), BF16),
            pltpu.VMEM((3, NB, BS, 2 * E), BF16),
            pltpu.VMEM((3, NB, BS, E), F32),
            pltpu.VMEM((3, NB, KP, BS), F32),
            pltpu.VMEM((3, NB, 24, E), jnp.int32),
            pltpu.VMEM((2, 2, NB, 1, E), jnp.int32),
            pltpu.VMEM((2, NB, KP, BS), BF16),
            pltpu.VMEM((2, NB, KP, BS), BF16),
            pltpu.VMEM((ng, share, E), F32),
            pltpu.VMEM((ng, share, E), F32),
            pltpu.VMEM((nz, share, E), F32),
            pltpu.VMEM((team, share, E), F32),
            pltpu.VMEM((2, share, E), F32),
            pltpu.SemaphoreType.DMA((NB, 4)),
            pltpu.SemaphoreType.DMA((2, steps)),
            pltpu.SemaphoreType.DMA((2, steps)),
            pltpu.SemaphoreType.DMA((2, NB)),
            pltpu.SemaphoreType.DMA((2, NB)),
            pltpu.SemaphoreType.DMA((3,)),
            pltpu.SemaphoreType.DMA((3,)),
            pltpu.SemaphoreType.REGULAR((3,)),
        ],
        compiler_params=pltpu.CompilerParams(
            collective_id=0, has_side_effects=True, vmem_limit_bytes=32 * 1024 * 1024
        ),
        name="walk",
    )(
        *(
            pltpu.with_memory_space_constraint(each, pltpu.HBM)
            for each in (points, start_panel, seventh, jnp.swapaxes(neighbours, 1, 2), counts)
        )
    )
    root = math.sqrt(pts * nb * ng)
    return pl.pallas_call(
        functools.partial(solve_kernel, root),
        out_shape=(
            jax.ShapeDtypeStruct((1, K, pts), F32),
            jax.ShapeDtypeStruct((K, K), F32),
        ),
        in_specs=[vmem, vmem],
        out_specs=(vmem, vmem),
        compiler_params=pltpu.CompilerParams(vmem_limit_bytes=16 * 1024 * 1024),
        name="solve",
    )(gram, walked)


def solution(mesh):
    in_specs = (
        P("grp", "blk", None),
        P("grp", None, "blk"),
        P("grp", "blk"),
        P("grp", None, None),
        P("grp", None),
    )
    out_specs = (P("grp", None, "blk"), P())
    return jax.shard_map(local, mesh=mesh, in_specs=in_specs, out_specs=out_specs, check_vma=False)
```

```python
import functools
import math

import jax
import jax.numpy as jnp
from jax import lax
from jax.experimental import pallas as pl
from jax.experimental.pallas import tpu as pltpu
from jax.sharding import PartitionSpec as P

E = 128
K = 64
BS = 256
SLOTS = 16
NB = 4
ROWS = BS + 2 * K + 8
KP = K + 8
LOG2E = 1.4426950408889634
MESH = pl.DeviceIdType.MESH
F32 = jnp.float32
BF16 = jnp.bfloat16


def nt_dot(a, b, precision=None):
    return lax.dot_general(
        a, b, (((1,), (1,)), ((), ())), precision=precision, preferred_element_type=F32
    )


def split3(value):
    hi = value.astype(BF16).astype(F32)
    mid = (value - hi).astype(BF16).astype(F32)
    return hi, mid, value - hi - mid


def far_slots(listed):
    f0, f1, f2, f3 = listed
    n0, n1, n2, n3 = 1 - f0, 1 - f1, 1 - f2, 1 - f3
    first = (f0, n0 * f1, n0 * n1 * f2 * f3, jnp.zeros_like(f0))
    second = (jnp.zeros_like(f0), n3 * n2 * f1 * f0, n3 * f2, f3)
    return first, second


def walk_kernel(
    sizes, pts, pan, sev_in, lists_in, counts_in, walked, gram_out,
    sev, lists, counts, own, recv, stage, xaug, apcol, acc, mask, pick, rout, rin, g3, s0, s1, s2, p3,
    isem, ssem, rsem, osem, nsem, asend, arecv, heard,
):
    nb, ng, nz = sizes
    nx = nb // nz
    near = 2 * NB
    steps = near + 2
    me = lax.axis_index("blk")
    mg = lax.axis_index("grp")
    right = lax.rem(me + 1, nb)
    left = lax.rem(me + nb - 1, nb)
    zz = lax.rem(me, nz)
    xx = me // nz
    team = nx * ng
    rank = xx * ng + mg

    yy = mg // 2
    core = lax.rem(mg, 2)
    ny = ng // 2

    def team_peer(o):
        gx = lax.rem(xx + o[0], nx)
        gg = lax.rem(yy + o[1], ny) * 2 + lax.rem(core + o[2], 2)
        return (gx * nz + zz, gg), gx * ng + gg

    def line_peer(o):
        return (xx * nz + lax.rem(zz + o, nz), mg)

    def away_by(o, size):
        return min(o, size - o)

    team_offsets = [(a, b, c) for a in range(nx) for b in range(ny) for c in range(2)][1:]
    team_offsets.sort(key=lambda o: (-away_by(o[0], nx) - away_by(o[1], ny), o))
    line_offsets = sorted(range(1, nz), key=lambda o: (-away_by(o, nz), o))

    small = [
        pltpu.make_async_copy(sev_in, sev, isem.at[0, 3]),
        pltpu.make_async_copy(lists_in.at[0], lists, isem.at[1, 3]),
        pltpu.make_async_copy(counts_in, counts, isem.at[2, 3]),
    ]
    small[0].start()
    loads = []
    for b in range(NB):
        low = b * BS
        loads.append(
            [
                pltpu.make_async_copy(pts.at[0, low : low + BS, :], own.at[b, 0:BS, :], isem.at[b, 0]),
                pltpu.make_async_copy(
                    pan.at[0, :, low : low + E], own.at[b, BS : BS + K, :], isem.at[b, 1]
                ),
                pltpu.make_async_copy(
                    pan.at[0, :, low + E : low + BS], own.at[b, BS + K : BS + 2 * K, :], isem.at[b, 2]
                ),
            ]
        )
    for load in loads[0]:
        load.start()

    next_to = [line_peer(1), line_peer(nz - 1)]
    next_to += [team_peer(o)[0] for o in ((1, 0, 0), (nx - 1, 0, 0), (0, 1, 0), (0, ny - 1, 0), (0, 0, 1))]
    partners = [(right, mg), (left, mg)] + next_to
    rounds = [
        next_to,
        [line_peer(2), line_peer(nz - 2)]
        + [team_peer(o)[0] for o in ((2, 0, 0), (0, 2, 0), (1, 0, 0), (nx - 1, 0, 0))],
        [line_peer(4), line_peer(nz - 4), team_peer((0, 0, 1))[0]],
    ]

    def vouch(at):
        for partner in rounds[at]:
            pl.semaphore_signal(heard.at[at], inc=1, device_id=partner, device_id_type=MESH)

    def hear(at):
        pl.semaphore_wait(heard.at[at], len(rounds[at]))

    barrier = pltpu.get_barrier_semaphore()
    for partner in partners:
        pl.semaphore_signal(barrier, inc=1, device_id=partner, device_id_type=MESH)
    for b in range(1, NB):
        for load in loads[b]:
            load.start()
    small[1].start()
    small[2].start()

    lane = lax.broadcasted_iota(jnp.int32, (BS, E), 1)

    def prepare(b):
        for load in loads[b]:
            load.wait()
        x = own[b, 0:BS, :]
        xf = x.astype(F32)
        place = jnp.broadcast_to(sev[0:1, b * BS : (b + 1) * BS].astype(F32), (E, BS)).T
        place = jnp.concatenate([place, place], axis=1).astype(jnp.int32)
        picked = (place == lax.broadcasted_iota(jnp.int32, (BS, BS), 1)).astype(F32).astype(BF16)
        partner = jnp.dot(picked, x, preferred_element_type=F32)
        diff = xf - partner
        scale = jnp.sqrt(jnp.sum(diff * diff, axis=1, keepdims=True) + 1e-06)
        scale = jnp.broadcast_to(scale, (BS, E)).astype(BF16).astype(F32)
        norm = jnp.broadcast_to(jnp.sum(xf * xf, axis=1, keepdims=True), (BS, E))
        hi, mid, low = split3(norm)
        zero = jnp.zeros_like(norm)
        columns = jnp.where(
            lane == 0, hi, jnp.where(lane == 1, mid, jnp.where(lane == 2, low, jnp.where(lane == 3, scale, zero)))
        )
        stats = columns.T[0:4, :]
        own[b, BS + 2 * K : ROWS, :] = jnp.concatenate([stats[:, :E], stats[:, E:]], axis=0).astype(BF16)
        keep_rows(0, b, xf, columns, scale)

    def keep_rows(who, b, xf, columns, scale):
        xaug[who, b, :, 0:E] = (2.0 * xf).astype(BF16)
        xaug[who, b, :, E : 2 * E] = jnp.where(lane < 3, -columns, 0.0).astype(BF16)
        apcol[who, b, :, :] = LOG2E / scale

    def row_stats(slab):
        stats = slab[BS + 2 * K : ROWS, :].astype(F32)
        return jnp.concatenate([stats[0:4, :], stats[4:8, :]], axis=1)

    def adopt(who, b, slab):
        columns = jnp.concatenate([row_stats(slab)] * (E // 4), axis=0).T
        keep_rows(who, b, slab[0:BS, :].astype(F32), columns, jnp.broadcast_to(columns[:, 3:4], (BS, E)))

    def hop(d, slot, source):
        return pltpu.make_async_remote_copy(
            src_ref=source,
            dst_ref=recv.at[d, slot],
            send_sem=ssem.at[d, slot],
            recv_sem=rsem.at[d, slot],
            device_id=((right, left)[d], mg),
            device_id_type=MESH,
        )

    small[0].wait()
    prepare(0)
    pl.semaphore_wait(barrier, len(partners))
    for b in range(NB):
        if b:
            prepare(b)
        for d in range(2):
            hop(d, b, own.at[b]).start()
    vouch(0)
    small[1].wait()
    small[2].wait()

    def wrapped(owner):
        return jnp.where(owner < 0, owner + nb, jnp.where(owner >= nb, owner - nb, owner))

    def found_in(ids, row, found):
        for s in range(SLOTS):
            entry = jnp.where(s < counts[0, row], lists[s, row], -1)
            found = jnp.where(ids == entry, 1, found)
        return found

    spot = lax.broadcasted_iota(jnp.int32, (mask.shape[2], E), 0)
    away = spot - NB
    dist = lax.shift_right_arithmetic(jnp.where(away >= near, away - near, away), 2) + 1
    shift = jnp.where(spot < NB, 0, jnp.where(away >= near, dist, -dist))
    ids = wrapped(me + shift) * NB + (spot & (NB - 1))
    for r in range(NB):
        mask[0, r, :, :] = found_in(ids, me * NB + r, jnp.zeros(ids.shape, jnp.int32))
    sub = lax.broadcasted_iota(jnp.int32, (8, E), 0)
    for d in range(2):
        toward = (right, left)[d]
        side = 2 * d - 1
        ids = wrapped(me + jnp.where(sub < NB, 2 * side, 3 * side)) * NB + (sub & (NB - 1))
        founds = [found_in(ids, toward * NB + r, jnp.zeros((8, E), jnp.int32)) for r in range(NB)]
        rows = [[f[NB + c : NB + c + 1, :] for c in range(NB)] for f in founds]
        listed = [functools.reduce(jnp.maximum, [row[c] for row in rows]) for c in range(NB)]
        for r in range(NB):
            mask[1 + d, r, 0:8, :] = founds[r]
            for at, chosen in enumerate(far_slots(listed)):
                mask[1 + d, r, NB + at : NB + at + 1, :] = sum(chosen[c] * rows[r][c] for c in range(NB))
        blocks = wrapped(me + 2 * side) * NB + sub
        found = jnp.zeros((8, E), jnp.int32)
        for r in range(NB):
            found = found_in(blocks, wrapped(me - 2 * side) * NB + r, found)
        for at, chosen in enumerate(far_slots([found[c : c + 1, :] for c in range(NB)])):
            for c in range(NB):
                pick[d, at, c, :, :] = chosen[c]

    acc[...] = jnp.zeros_like(acc)
    stage[...] = jnp.zeros_like(stage)
    tail = (lane < 3).astype(F32).astype(BF16)
    ones = jnp.ones((KP - K, BS), BF16)

    def block(slab, who, spot_index):
        keys = jnp.concatenate([slab[0:BS, :], tail], axis=1)
        panel = jnp.concatenate([slab[BS : BS + K, :], slab[BS + K : BS + 2 * K, :]], axis=1)
        panel = jnp.concatenate([panel, ones], axis=0)
        stats = row_stats(slab)
        aq = 1.0 / stats[3:4, :]
        nq = stats[0:1, :] + stats[1:2, :] + stats[2:3, :]
        for r in range(NB):
            cross = nt_dot(xaug[who, r], keys)
            ap = apcol[who, r]
            power = ((cross - nq) * aq) * jnp.concatenate([ap, ap], axis=1)
            weights = jnp.exp2(power).astype(BF16)
            carried = nt_dot(panel, weights)
            live = mask[who, r, pl.ds(spot_index, 1), :]
            live = jnp.concatenate([live, live], axis=1)
            acc[who, r, :, :] += jnp.where(live > 0, carried, 0.0)

    def inside(b, carry):
        block(own.at[b], 0, b)
        return carry

    lax.fori_loop(0, NB, inside, 0)

    def first_hop(t, carry):
        for d in range(2):
            hop(d, t, recv.at[d, t]).wait_recv()
            hop(d, t + NB, recv.at[d, t]).start()

        @pl.when(t == NB - 1)
        def _():
            hear(0)
            vouch(1)

        for d in range(2):
            block(recv.at[d, t], 0, NB + d * near + t)
            adopt(2 - d, t, recv.at[d, t])
        return carry

    lax.fori_loop(0, NB, first_hop, 0)

    def second_hop(c, carry):
        t = c + NB
        for d in range(2):
            hop(d, t, recv.at[d, t]).wait_recv()
            for at, (low, high) in enumerate(((0, 2), (1, 3))):

                @pl.when(jnp.logical_and(c >= low, c <= high))
                def _():
                    wanted = pick[d, at, c]
                    kept = stage[d, at].astype(F32)
                    taken = jnp.where(wanted > 0, recv[d, t].astype(F32), kept)
                    stage[d, at] = taken.astype(BF16)

                @pl.when(c == high)
                def _():
                    hop(d, near + at, stage.at[d, at]).start()

        @pl.when(c == 2)
        def _():
            hear(1)
            vouch(2)

        for d in range(2):
            block(recv.at[d, t], 1 + d, c)
        return carry

    lax.fori_loop(0, NB, second_hop, 0)

    def third_hop(at, carry):
        for d in range(2):
            hop(d, near + at, recv.at[d, near + at]).wait_recv()
        for d in range(2):
            block(recv.at[d, near + at], 1 + d, NB + at)
        return carry

    lax.fori_loop(0, 2, third_hop, 0)

    def result(d, r):
        return pltpu.make_async_remote_copy(
            src_ref=rout.at[d, r],
            dst_ref=rin.at[d, r],
            send_sem=osem.at[d, r],
            recv_sem=nsem.at[d, r],
            device_id=((right, left)[d], mg),
            device_id_type=MESH,
        )

    rest = lax.broadcasted_iota(jnp.int32, (KP - K, BS), 0)
    for r in range(NB):
        for d in range(2):
            degree = acc[1 + d, r, K:KP, :]
            high = degree.astype(BF16).astype(F32)
            degree = jnp.where(rest == 0, high, jnp.where(rest == 1, degree - high, 0.0))
            rout[d, r, 0:K, :] = acc[1 + d, r, 0:K, :].astype(BF16)
            rout[d, r, K:KP, :] = degree.astype(BF16)
            result(d, r).start()

    def own_rows_later(t, carry):
        for d in range(2):
            block(recv.at[d, t], 0, NB + d * near + t)
        return carry

    lax.fori_loop(NB, near, own_rows_later, 0)
    hear(2)

    for r in range(NB):
        cols = slice(r * BS, (r + 1) * BS)
        total = acc[0, r, 0 : K + 8, :]
        for d in range(2):
            result(d, r).wait_recv()
            more = rin[d, r, :, :].astype(F32)
            extra = more[K : K + 1, :] + more[K + 1 : K + 2, :]
            total = total + jnp.concatenate([more[0:K, :], jnp.broadcast_to(extra, (8, BS))], axis=0)
        panel = jnp.concatenate([own[r, BS : BS + K, :], own[r, BS + K : BS + 2 * K, :]], axis=1)
        walked[:, cols] = (panel.astype(F32) + total[0:K, :]) / (1.0 + total[K : K + 1, :])
    flat = walked[...]
    gram = nt_dot(flat, jnp.concatenate([flat, flat], axis=0), lax.Precision.HIGHEST)
    half = lax.broadcasted_iota(jnp.int32, (K // 2, E), 1) < K
    packed = jnp.where(half, gram[0 : K // 2, :], gram[K // 2 : K, :])

    def sent(t, carry):
        for d in range(2):
            hop(d, t, recv.at[d, t]).wait_send()
        return carry

    for d in range(2):
        for r in range(NB):
            result(d, r).wait_send()

    share = K // 2 // ng
    grp_offsets = [o for o in team_offsets if o[0] == 0]

    def exchange(at, offsets, source, target, slot, peer):
        for o in offsets:
            pltpu.make_async_remote_copy(
                src_ref=source(o),
                dst_ref=target.at[slot],
                send_sem=asend.at[at],
                recv_sem=arecv.at[at],
                device_id=peer(o),
                device_id_type=MESH,
            ).start()

    def arrived(at, size, target):
        whole = target.at[pl.ds(0, size - 1)]
        return pltpu.make_async_remote_copy(
            src_ref=whole,
            dst_ref=whole,
            send_sem=asend.at[at],
            recv_sem=arecv.at[at],
            device_id=line_peer(1),
            device_id_type=MESH,
        )

    for i in range(ng):
        g3[i] = packed[i * share : (i + 1) * share, :]
    exchange(
        0, grp_offsets, lambda o: g3.at[team_peer(o)[0][1]], s0, mg, lambda o: team_peer(o)[0]
    )
    s0[mg] = g3[mg]
    lax.fori_loop(0, steps, sent, 0)
    arrived(0, ng, s0).wait_recv()
    p3[0] = jnp.sum(s0[...], axis=0)
    exchange(1, line_offsets, lambda o: p3.at[0], s1, zz, line_peer)
    s1[zz] = p3[0]
    arrived(1, nz, s1).wait_recv()
    p3[1] = jnp.sum(s1[...], axis=0)
    exchange(2, team_offsets, lambda o: p3.at[1], s2, rank, lambda o: team_peer(o)[0])
    s2[rank] = p3[1]
    arrived(2, team, s2).wait_recv()
    whole = []
    for i in range(ng):
        part = s2[i]
        for x in range(1, nx):
            part = part + s2[x * ng + i]
        whole.append(part)
    whole = jnp.concatenate(whole, axis=0)
    gram_out[0 : K // 2, :] = jnp.where(half, whole, 0.0)
    gram_out[K // 2 : K, :] = jnp.where(half, pltpu.roll(whole, K, 1), 0.0)
    arrived(0, ng, s0).wait_send()
    arrived(1, nz, s1).wait_send()
    arrived(2, team, s2).wait_send()


def solve_kernel(root, gram, walked, ortho, r_factor):
    group = 8
    count = K // group
    sub = lax.broadcasted_iota(jnp.int32, (group, E), 0)
    col = lax.broadcasted_iota(jnp.int32, (group, E), 1)
    tiles = []
    for i in range(count):
        unit = (col == sub + (K + i * group)).astype(F32)
        tiles.append(gram[i * group : (i + 1) * group, :] + unit)
    for at in range(count):
        base = at * group
        wide = {
            i: [jnp.broadcast_to(tiles[i][:, base + k : base + k + 1], (group, E)) for k in range(group)]
            for i in range(at, count)
        }
        for k in range(group):
            inverse = 1.0 / wide[at][k][k : k + 1, :]
            row = tiles[at][k : k + 1, :] * inverse
            later = {m: wide[at][m][k : k + 1, :] * inverse for m in range(k + 1, group)}
            for i in range(at, count):
                factor = wide[i][k]
                if i == at:
                    factor = jnp.where(sub > k, factor, 0.0)
                tiles[i] = tiles[i] - factor * row
                for m, value in later.items():
                    wide[i][m] = wide[i][m] - factor * value
    rows = []
    for i in range(count):
        diagonal = jnp.sum(jnp.where(col == sub + i * group, tiles[i], 0.0), axis=1, keepdims=True)
        scaled = tiles[i] * (1.0 / jnp.sqrt(diagonal))
        upper = jnp.where(col >= sub + i * group, scaled, 0.0)
        r_factor[i * group : (i + 1) * group, :] = upper[:, 0:K] * (1.0 / root)
        rows.append(scaled[:, K : 2 * K] * root)
    ortho[0, :, :] = jnp.dot(
        jnp.concatenate(rows, axis=0),
        walked[...],
        precision=lax.Precision.HIGHEST,
        preferred_element_type=F32,
    )


def local(points, start_panel, seventh, neighbours, counts):
    nb = lax.axis_size("blk")
    ng = lax.axis_size("grp")
    nz = max(nb // 4, 1)
    pts = points.shape[1]
    team = (nb // nz) * ng
    share = K // 2 // ng
    steps = 2 * NB + 2
    vmem = pl.BlockSpec(memory_space=pltpu.VMEM)
    hbm = pl.BlockSpec(memory_space=pltpu.HBM)
    walked, gram = pl.pallas_call(
        functools.partial(walk_kernel, (nb, ng, nz)),
        out_shape=(
            jax.ShapeDtypeStruct((K, pts), F32),
            jax.ShapeDtypeStruct((K, E), F32),
        ),
        in_specs=[hbm] * 5,
        out_specs=(vmem, vmem),
        scratch_shapes=[
            pltpu.VMEM((1, pts), jnp.int32),
            pltpu.SMEM(neighbours.shape[:0:-1], jnp.int32),
            pltpu.SMEM(counts.shape, jnp.int32),
            pltpu.VMEM((NB, ROWS, E), BF16),
            pltpu.VMEM((2, steps, ROWS, E), BF16),
            pltpu.VMEM((2, 2, ROWS, E), BF16),
            pltpu.VMEM((3, NB, BS, 2 * E), BF16),
            pltpu.VMEM((3, NB, BS, E), F32),
            pltpu.VMEM((3, NB, KP, BS), F32),
            pltpu.VMEM((3, NB, 24, E), jnp.int32),
            pltpu.VMEM((2, 2, NB, 1, E), jnp.int32),
            pltpu.VMEM((2, NB, KP, BS), BF16),
            pltpu.VMEM((2, NB, KP, BS), BF16),
            pltpu.VMEM((ng, share, E), F32),
            pltpu.VMEM((ng, share, E), F32),
            pltpu.VMEM((nz, share, E), F32),
            pltpu.VMEM((team, share, E), F32),
            pltpu.VMEM((2, share, E), F32),
            pltpu.SemaphoreType.DMA((NB, 4)),
            pltpu.SemaphoreType.DMA((2, steps)),
            pltpu.SemaphoreType.DMA((2, steps)),
            pltpu.SemaphoreType.DMA((2, NB)),
            pltpu.SemaphoreType.DMA((2, NB)),
            pltpu.SemaphoreType.DMA((3,)),
            pltpu.SemaphoreType.DMA((3,)),
            pltpu.SemaphoreType.REGULAR((3,)),
        ],
        compiler_params=pltpu.CompilerParams(
            collective_id=0, has_side_effects=True, vmem_limit_bytes=32 * 1024 * 1024
        ),
        name="walk",
    )(
        *(
            pltpu.with_memory_space_constraint(each, pltpu.HBM)
            for each in (points, start_panel, seventh, jnp.swapaxes(neighbours, 1, 2), counts)
        )
    )
    root = math.sqrt(pts * nb * ng)
    return pl.pallas_call(
        functools.partial(solve_kernel, root),
        out_shape=(
            jax.ShapeDtypeStruct((1, K, pts), F32),
            jax.ShapeDtypeStruct((K, K), F32),
        ),
        in_specs=[vmem, vmem],
        out_specs=(vmem, vmem),
        compiler_params=pltpu.CompilerParams(vmem_limit_bytes=16 * 1024 * 1024),
        name="solve",
    )(gram, walked)


def solution(mesh):
    in_specs = (
        P("grp", "blk", None),
        P("grp", None, "blk"),
        P("grp", "blk"),
        P("grp", None, None),
        P("grp", None),
    )
    out_specs = (P("grp", None, "blk"), P())
    return jax.shard_map(local, mesh=mesh, in_specs=in_specs, out_specs=out_specs, check_vma=False)
```
